32 devices in a mesh: wide: 8 (over z, x), grp: 4 (over y, core).
Axes of the slice: x: 2, y: 2, z: 4, core: 2. Of those that a mesh axis runs over, the one named last changes fastest.
Arguments:
- query_rows: bfloat16 [4096, 1280], P(('wide', 'grp')), may hold values from -9 to 9, as said below
- key_rows: bfloat16 [4096, 1280], P(('wide', 'grp')), may hold values from -9 to 9, as said below
- value_rows: bfloat16 [4096, 1280], P(('wide', 'grp')), may hold values from -6 to 6
- block_image: int32 [32], replicated, may hold values from 0 to 6, never falling along the last dimension, each value on 1 to 8 neighbouring positions
Outputs:
- attended: bfloat16 [4096, 1280], P(('wide', 'grp'))
The draws below stay inside these ranges and needn't reach their ends.
Inputs may be any that keep to these rules, and one draw needn't show every extreme that they name: `query_rows`: Queries: entries bounded as stated. `key_rows`: Keys: entries bounded as stated. `block_image`: image numbers never fall along the window; every image covers 1 to 8 whole blocks and one covers exactly 8.
All inputs are finite; a program needn't handle non-finite values.
Results may differ from the reference program's by a relative error of at most 0.004.
Values may be sent and summed in bfloat16 or wider, within the bound.
A program may use at most 64 MiB of HBM per device.

```python
import math
import jax
import jax.numpy as jnp
import numpy as np
from jax import lax

HEADS = 16
HDIM = 80
BLK = 128
MOST = 8
NBLK = 32
TOKENS = 4096
IMAGES = 7


def plant_pair(key):
    width = HEADS * HDIM
    queries = jnp.clip(1.5 * jax.random.normal(jax.random.fold_in(key, 7), (TOKENS, width)), -9.0, 9.0)
    key_table = jnp.clip(1.5 * jax.random.normal(jax.random.fold_in(key, 8), (TOKENS, width)), -9.0, 9.0)
    return (queries.astype(jnp.float32), key_table.astype(jnp.float32))


def draw_query_rows(key, part):
    return plant_pair(key)[0].astype(jnp.bfloat16)


def draw_key_rows(key, part):
    return plant_pair(key)[1].astype(jnp.bfloat16)


def level_of(own_key, dims, shards, smallest, largest):
    gain, own = 1.0, jax.random.fold_in(own_key, 6)
    for position, shards_of in shards:
        heights = jnp.exp(jax.random.uniform(jax.random.fold_in(own, position), (shards_of,), jnp.float32, smallest / len(shards), largest / len(shards)))
        gain = gain * jnp.repeat(heights, dims[position] // shards_of).reshape([-1 if axis == position else 1 for axis in range(len(dims))])
    return gain


def profile(count, total, limit, lean):
    weights = [(1 << 20) // math.isqrt(standing ** lean) + 1 for standing in range(2, count + 1)]
    rest, holding = total - limit - (count - 1), [1] * (count - 1)
    while rest > 0:
        candidates = [i for i in range(count - 1) if holding[i] < limit]
        whole, remaining = sum([weights[i] for i in candidates]), rest
        for i in candidates:
            addition = min(limit - holding[i], max(1, remaining * weights[i] // whole), rest)
            holding[i] = holding[i] + addition
            rest = rest - addition
    return np.array([limit] + holding)


def uneven(stream_key, amount, total, most, slope):
    if amount == 2:
        one = jax.random.randint(stream_key, (), max(1, total - most), min(most, total - 1) + 1)
        return jnp.stack([one, total - one])
    sizes = jnp.asarray(profile(amount, total, most, slope), jnp.int32)
    twos = (amount - 1) // 2
    giver, sink = sizes[1:1 + 2 * twos:2], sizes[2:2 + 2 * twos:2]
    room = jnp.minimum(giver - 1, most - sink)
    moved = jax.random.randint(jax.random.fold_in(stream_key, 1), (twos,), 0, 1 << 20) % (room + 1)
    sizes = sizes.at[1:1 + 2 * twos:2].set(giver - moved).at[2:2 + 2 * twos:2].set(sink + moved)
    return sizes[jax.random.permutation(jax.random.fold_in(stream_key, 2), amount)]


def bell_draw(own_key, extent, scale, limit, shards=(), held_as=jnp.bfloat16):
    gain = level_of(own_key, extent, shards, -0.22, 0.18) if shards else 1.0
    values = jax.random.normal(own_key, extent, jnp.float32) * scale * gain
    return jnp.minimum(jnp.maximum(values, -limit), limit).astype(held_as)


def setup_inputs(seed: int = 0) -> dict:
    arg_keys = jax.random.split(jax.random.key(seed), 5)
    query_rows = draw_query_rows(jax.random.fold_in(arg_keys[4], 71), 0)
    key_rows = draw_key_rows(jax.random.fold_in(arg_keys[4], 71), 0)
    value_rows = bell_draw(arg_keys[2], (TOKENS, HEADS * HDIM), 1.0, 6.0, ((0, 32),))
    block_image = jnp.searchsorted(jnp.cumsum(uneven(arg_keys[3], IMAGES, NBLK, MOST, 1)), jnp.arange(NBLK), side="right").astype(jnp.int32)
    return {"query_rows": query_rows, "key_rows": key_rows, "value_rows": value_rows, "block_image": block_image}


neg_large = -1e+30

def reference(query_rows, key_rows, value_rows, block_image):
    margin = (MOST - 1) * BLK
    span_rows = BLK + 2 * margin
    token_ids = jnp.broadcast_to(block_image[:, None], (NBLK, BLK)).reshape(-1).astype(jnp.int32)
    padded_ids = jnp.pad(token_ids, (margin, margin), constant_values=-1)
    padded_keys = jnp.pad(key_rows.reshape(TOKENS, HEADS, HDIM), ((margin, margin), (0, 0), (0, 0)))
    padded_values = jnp.pad(value_rows.reshape(TOKENS, HEADS, HDIM), ((margin, margin), (0, 0), (0, 0)))
    query_heads = query_rows.reshape(NBLK, BLK, HEADS, HDIM)
    scale_value = 1.0 / math.sqrt(HDIM)

    def one_block(block_index):
        first_row = (block_index * BLK).astype(jnp.int32)
        query_block = lax.dynamic_index_in_dim(query_heads, block_index, 0, keepdims=False).astype(jnp.float32)
        key_window = lax.dynamic_slice_in_dim(padded_keys, first_row, span_rows, 0).astype(jnp.float32)
        value_window = lax.dynamic_slice_in_dim(padded_values, first_row, span_rows, 0).astype(jnp.float32)
        id_window = lax.dynamic_slice_in_dim(padded_ids, first_row, span_rows, 0)
        query_ids = lax.dynamic_slice_in_dim(token_ids, first_row, BLK, 0)
        same_image = query_ids[:, None] == id_window[None, :]
        scores = jnp.einsum('qhd,khd->hqk', query_block, key_window) * scale_value
        scores = jnp.where(same_image[None], scores, neg_large)
        row_max = lax.optimization_barrier(jnp.max(scores, axis=-1, keepdims=True))
        weights = jnp.where(same_image[None], jnp.exp(scores - row_max), 0.0)
        denominator = lax.optimization_barrier(jnp.sum(weights, axis=-1))
        rounded = lax.optimization_barrier(weights.astype(jnp.bfloat16)).astype(jnp.float32)
        attended = jnp.einsum('hqk,khd->qhd', rounded, value_window) / jnp.transpose(denominator)[:, :, None]
        return attended.reshape(BLK, HEADS * HDIM).astype(jnp.bfloat16)
    blocks = lax.map(one_block, jnp.arange(NBLK, dtype=jnp.int32))
    return blocks.reshape(TOKENS, HEADS * HDIM)
```

```python
import functools
import math

import jax
import jax.numpy as jnp
from jax import lax
from jax.experimental import pallas as pl
from jax.experimental.pallas import tpu as pltpu
from jax.sharding import PartitionSpec as P

HDIM = 80
BLK = 128
MOST = 8
NEG = -1e30
MESH = pl.DeviceIdType.MESH


def kernel(cfg, img_hbm, q_hbm, k_hbm, v_hbm, out, img, q_in, k_in, v_in, k_src, q_src, v_src,
           k_own, q_own, v_own, k_halo, v_halo, kn, vt, l_scr, s_scr, p_scr, o_src, o_own,
           load_s, k_rs, q_rs, v_rs, o_rs, send_s, halo_ss, halo_rs, keep_s):
    planes, fold, grp, heads = cfg
    n = fold * grp
    cols = heads * HDIM
    pairs = n // 2
    wide_at, grp_at = lax.axis_index("wide"), lax.axis_index("grp")
    plane = wide_at // fold
    fold_at = wide_at % fold
    me = fold_at * grp + grp_at
    mine = me // 2
    mate = mine * 2 + 1 - me % 2
    has_prev, has_next = plane > 0, plane < planes - 1

    loads = [pltpu.make_async_copy(src, dst, load_s.at[i])
             for i, (src, dst) in enumerate(((k_hbm, k_in), (q_hbm, q_in), (v_hbm, v_in), (img_hbm, img)))]
    for load in loads:
        load.start()
    def device(at_plane, member):
        return (at_plane * fold + member // grp, member % grp)

    barrier = pltpu.get_barrier_semaphore()
    for i in range(1, n):
        pl.semaphore_signal(barrier, inc=1, device_id=device(plane, (me + i) % n), device_id_type=MESH)

    @pl.when(has_prev)
    def _():
        pl.semaphore_signal(barrier, inc=1, device_id=device(plane - 1, me), device_id_type=MESH)

    @pl.when(has_next)
    def _():
        pl.semaphore_signal(barrier, inc=1, device_id=device(plane + 1, me), device_id_type=MESH)

    @pl.when(jnp.logical_not(has_prev))
    def _():
        for ref in (kn, vt):
            ref[0:n - 1] = jnp.zeros((n - 1,) + ref.shape[1:], ref.dtype)

    @pl.when(jnp.logical_not(has_next))
    def _():
        for ref in (kn, vt):
            ref[2 * n - 1:3 * n - 2] = jnp.zeros((n - 1,) + ref.shape[1:], ref.dtype)
    def turn(ref, dst):
        whole = jnp.concatenate([ref[:, c:c + BLK].T for c in range(0, n * cols, BLK)], axis=0)
        for member in range(n):
            dst[member] = whole[member * cols:(member + 1) * cols]

    def remote(src, dst, ss, rs, dev):
        return pltpu.make_async_remote_copy(src_ref=src, dst_ref=dst, send_sem=ss, recv_sem=rs,
                                            device_id=dev, device_id_type=MESH)

    def exchange(src, dst, ss, rs):
        def send(to):
            remote(src.at[to], dst.at[me], ss, rs.at[mine], device(plane, to)).start()

        def take(pair):
            remote(src.at[pl.ds(0, 2)], dst.at[pl.ds(2 * pair, 2)], ss, rs.at[pair], device(plane, mate)).wait_recv()

        def take_mate():
            remote(src.at[0], dst.at[mate], ss, rs.at[mine], device(plane, mate)).wait_recv()

        def sent():
            part = src.at[pl.ds(0, n - 1)]
            remote(part, part, ss, rs.at[0], device(plane, mate)).wait_send()
        return send, take, take_mate, sent

    k_send, k_take, k_mate, k_sent = exchange(k_src, k_own, send_s.at[0], k_rs)
    q_send, q_take, q_mate, q_sent = exchange(q_src, q_own, send_s.at[1], q_rs)
    v_send, v_take, v_mate, v_sent = exchange(v_src, v_own, send_s.at[2], v_rs)

    def forward(which, halo, member, src):
        @pl.when(jnp.logical_and(has_next, member >= 1))
        def _():
            remote(src, halo.at[member - 1], halo_ss.at[which, 0], halo_rs.at[which, 0],
                   device(plane + 1, me)).start()

        @pl.when(jnp.logical_and(has_prev, member <= n - 2))
        def _():
            remote(src, halo.at[n - 1 + member], halo_ss.at[which, 1], halo_rs.at[which, 1],
                   device(plane - 1, me)).start()

    def take_below(which, halo):
        part = halo.at[pl.ds(0, n - 1)]
        remote(part, part, halo_ss.at[which, 0], halo_rs.at[which, 0], device(plane, mate)).wait_recv()

    def take_above(which, halo):
        part = halo.at[pl.ds(n - 1, n - 1)]
        remote(part, part, halo_ss.at[which, 1], halo_rs.at[which, 1], device(plane, mate)).wait_recv()

    def sent_up(which, halo):
        part = halo.at[pl.ds(0, n - 1)]
        remote(part, part, halo_ss.at[which, 0], halo_rs.at[which, 0], device(plane, mate)).wait_send()

    def sent_down(which, halo):
        part = halo.at[pl.ds(n - 1, n - 1)]
        remote(part, part, halo_ss.at[which, 1], halo_rs.at[which, 1], device(plane, mate)).wait_send()

    def out_order(send):
        for step in range(1, pairs):
            for r in range(2):
                send((mine + pairs - step) % pairs * 2 + r)

    loads[0].wait()
    turn(k_in, k_src)
    pl.semaphore_wait(barrier, n - 1 + has_prev.astype(jnp.int32) + has_next.astype(jnp.int32))
    forward(0, k_halo, me, k_src.at[me])
    k_send(mate)
    out_order(k_send)
    loads[2].wait()
    turn(v_in, v_src)
    forward(1, v_halo, me, v_src.at[me])
    v_send(mate)
    loads[1].wait()
    turn(q_in, q_src)
    q_send(mate)
    out_order(v_send)
    out_order(q_send)
    keep = pltpu.make_async_copy(q_src.at[me], q_own.at[me], keep_s.at[0])
    keep.start()
    def natural(slot, src):
        kn[slot] = src[...].T

    natural(n - 1 + me, k_src.at[me])
    vt[n - 1 + me] = v_src[me]
    k_mate()
    forward(0, k_halo, mate, k_own.at[mate])
    natural(n - 1 + mate, k_own.at[mate])
    def take_k(step, carry):
        pair = (mine + step) % pairs
        k_take(pair)
        for r in range(2):
            forward(0, k_halo, 2 * pair + r, k_own.at[2 * pair + r])
        for r in range(2):
            natural(n - 1 + 2 * pair + r, k_own.at[2 * pair + r])
        return carry

    lax.fori_loop(1, pairs, take_k, 0)
    v_mate()
    forward(1, v_halo, mate, v_own.at[mate])
    vt[n - 1 + mate] = v_own[mate]
    def take_v(step, carry):
        pair = (mine + step) % pairs
        v_take(pair)
        for r in range(2):
            forward(1, v_halo, 2 * pair + r, v_own.at[2 * pair + r])
        for r in range(2):
            vt[n - 1 + 2 * pair + r] = v_own[2 * pair + r]
        return carry

    lax.fori_loop(1, pairs, take_v, 0)
    def turn_below(i, carry):
        natural(i, k_halo.at[i])
        return carry

    def turn_above(i, carry):
        natural(n + i, k_halo.at[i])
        return carry

    @pl.when(has_prev)
    def _():
        take_below(0, k_halo)
        lax.fori_loop(0, n - 1, turn_below, 0)

    @pl.when(has_next)
    def _():
        take_above(0, k_halo)
        lax.fori_loop(n - 1, 2 * n - 2, turn_above, 0)
    loads[3].wait()
    factor = math.log2(math.e) / math.sqrt(HDIM)
    blocks = img.shape[0]
    base = plane * n

    def span(block):
        own_id = img[block]
        before, after = jnp.int32(0), jnp.int32(0)
        for d in range(1, MOST):
            low = jnp.where(block >= d, img[jnp.maximum(block - d, 0)], -1)
            high = jnp.where(block + d < blocks, img[jnp.minimum(block + d, blocks - 1)], -1)
            before += (low == own_id).astype(jnp.int32)
            after += (high == own_id).astype(jnp.int32)
        return before, before + after + 1

    def first_slot(m):
        before, count = span(base + m)
        return m + n - 1 - before, count

    def weights(m, slot):
        start, count = first_slot(m)
        rows = []
        for h in range(heads):
            q_h = q_own[m, h * HDIM:(h + 1) * HDIM]
            none = jnp.zeros_like(q_h)
            rows.append(jnp.concatenate([q_h if j == h else none for j in range(heads)], axis=1))
        q_all = jnp.concatenate(rows, axis=0)
        top = jnp.full((1, heads * BLK), NEG, jnp.float32)
        for t in range(MOST):
            s = jnp.dot(kn[start + t], q_all, preferred_element_type=jnp.float32)
            s_scr[slot, t] = s
            top = jnp.maximum(top, jnp.where(t < count, jnp.max(s, axis=0, keepdims=True), NEG))
        total = jnp.zeros((8, heads * BLK), jnp.float32)
        for t in range(MOST):
            shift = jnp.where(t < count, -top * factor, NEG)
            w = jnp.exp2(s_scr[slot, t] * factor + shift)
            total = total + jnp.sum(w.reshape(BLK // 8, 8, heads * BLK), axis=0)
            p_scr[m, t * BLK:(t + 1) * BLK] = w.astype(jnp.bfloat16)
        l_scr[m] = jnp.sum(total, axis=0, keepdims=True)

    def score(pair):
        for r in range(2):
            weights(2 * pair + r, r)

    def score_step(step, carry):
        pair = (mine + step) % pairs
        @pl.when(step == 0)
        def _():
            keep.wait()
            q_mate()
        @pl.when(step > 0)
        def _():
            q_take(pair)
        score(pair)
        return carry

    lax.fori_loop(0, pairs, score_step, 0)
    def move_below(i, carry):
        vt[i] = v_halo[i]
        return carry

    def move_above(i, carry):
        vt[n + i] = v_halo[i]
        return carry

    @pl.when(has_prev)
    def _():
        take_below(1, v_halo)
        lax.fori_loop(0, n - 1, move_below, 0)

    @pl.when(has_next)
    def _():
        take_above(1, v_halo)
        lax.fori_loop(n - 1, 2 * n - 2, move_above, 0)
    o_send, o_take, o_mate, o_sent = exchange(o_src, o_own, send_s.at[3], o_rs)

    def finish(step, carry):
        pair = (mine + 1 + step) % pairs
        for r in range(2):
            m = 2 * pair + r
            start, _ = first_slot(m)
            v = jnp.concatenate([vt[start + t] for t in range(MOST)], axis=1)
            res = jnp.dot(v, p_scr[m], preferred_element_type=jnp.float32)
            res = jnp.concatenate([res[h * HDIM:(h + 1) * HDIM, h * BLK:(h + 1) * BLK]
                                   / l_scr[m, :, h * BLK:(h + 1) * BLK] for h in range(heads)], axis=0)
            o_src[m] = res.astype(jnp.bfloat16)
        for r in range(2):
            m = 2 * pair + r

            @pl.when(m != me)
            def _():
                o_send(m)
        return carry

    lax.fori_loop(0, pairs, finish, 0)
    o_own[me] = o_src[me]
    k_sent()
    q_sent()
    v_sent()
    for which, halo in ((0, k_halo), (1, v_halo)):
        @pl.when(has_next)
        def _():
            sent_up(which, halo)

        @pl.when(has_prev)
        def _():
            sent_down(which, halo)
    o_mate()
    for step in range(1, pairs):
        o_take((mine + step) % pairs)
    flat = jnp.concatenate([o_own[member] for member in range(n)], axis=0)
    for c in range(0, n * cols, BLK):
        out[:, c:c + BLK] = flat[c:c + BLK].T
    o_sent()


def solution(mesh):
    wide, grp = mesh.shape["wide"], mesh.shape["grp"]
    fold = MOST // grp
    n = fold * grp
    planes = wide // fold

    def body(query_rows, key_rows, value_rows, block_image):
        rows, width = query_rows.shape
        heads = width // HDIM // n
        cols = heads * HDIM
        bf, f32 = jnp.bfloat16, jnp.float32
        hbm = pl.BlockSpec(memory_space=pltpu.HBM)
        dma = pltpu.SemaphoreType.DMA
        slices = pltpu.VMEM((n, cols, BLK), bf)
        halo = pltpu.VMEM((2 * n - 2, cols, BLK), bf)
        lanes = heads * BLK
        args = [pltpu.with_memory_space_constraint(a, pltpu.HBM)
                for a in (block_image, query_rows, key_rows, value_rows)]
        return pl.pallas_call(
            functools.partial(kernel, (planes, fold, grp, heads)),
            out_shape=jax.ShapeDtypeStruct((rows, width), bf),
            in_specs=[hbm] * 4,
            out_specs=pl.BlockSpec(memory_space=pltpu.VMEM),
            scratch_shapes=[pltpu.SMEM(block_image.shape, jnp.int32)]
            + [pltpu.VMEM((rows, width), bf)] * 3 + [slices] * 6 + [halo] * 2 + [
                pltpu.VMEM((3 * n - 2, BLK, cols), bf),
                pltpu.VMEM((3 * n - 2, cols, BLK), bf),
                pltpu.VMEM((n, 1, lanes), f32),
                pltpu.VMEM((2, MOST, BLK, lanes), f32),
                pltpu.VMEM((n, MOST * BLK, lanes), bf),
                slices, slices,
            ] + [dma((4,))] + [dma((n // 2,))] * 4 + [dma((4,)), dma((2, 2)), dma((2, 2)), dma((1,))],
            compiler_params=pltpu.CompilerParams(collective_id=0, has_side_effects=True,
                                                 vmem_limit_bytes=40 << 20),
        )(*args)

    return jax.shard_map(
        body,
        mesh=mesh,
        in_specs=(
            P(("wide", "grp"), None),
            P(("wide", "grp"), None),
            P(("wide", "grp"), None),
            P(),
        ),
        out_specs=P(("wide", "grp"), None),
        check_vma=False,
    )
```

```python
import functools
import math

import jax
import jax.numpy as jnp
from jax import lax
from jax.experimental import pallas as pl
from jax.experimental.pallas import tpu as pltpu
from jax.sharding import PartitionSpec as P

HDIM = 80
BLK = 128
MOST = 8
NEG = -1e30
MESH = pl.DeviceIdType.MESH


def kernel(cfg, img_hbm, q_hbm, k_hbm, v_hbm, out, img, q_in, k_in, v_in, k_src, q_src, v_src,
           k_own, q_own, v_own, k_halo, v_halo, kn, vt, l_scr, s_scr, p_scr, o_src, o_own,
           load_s, k_rs, q_rs, v_rs, o_rs, send_s, halo_ss, halo_rs, keep_s):
    planes, fold, grp, heads = cfg
    n = fold * grp
    cols = heads * HDIM
    pairs = n // 2
    wide_at, grp_at = lax.axis_index("wide"), lax.axis_index("grp")
    plane = wide_at // fold
    fold_at = wide_at % fold
    me = fold_at * grp + grp_at
    mine = me // 2
    mate = mine * 2 + 1 - me % 2
    has_prev, has_next = plane > 0, plane < planes - 1

    loads = [pltpu.make_async_copy(src, dst, load_s.at[i])
             for i, (src, dst) in enumerate(((k_hbm, k_in), (q_hbm, q_in), (v_hbm, v_in), (img_hbm, img)))]
    for load in loads:
        load.start()
    def device(at_plane, member):
        return (at_plane * fold + member // grp, member % grp)

    barrier = pltpu.get_barrier_semaphore()
    for i in range(1, n):
        pl.semaphore_signal(barrier, inc=1, device_id=device(plane, (me + i) % n), device_id_type=MESH)

    @pl.when(has_prev)
    def _():
        pl.semaphore_signal(barrier, inc=1, device_id=device(plane - 1, me), device_id_type=MESH)

    @pl.when(has_next)
    def _():
        pl.semaphore_signal(barrier, inc=1, device_id=device(plane + 1, me), device_id_type=MESH)

    @pl.when(jnp.logical_not(has_prev))
    def _():
        for ref in (kn, vt):
            ref[0:n - 1] = jnp.zeros((n - 1,) + ref.shape[1:], ref.dtype)

    @pl.when(jnp.logical_not(has_next))
    def _():
        for ref in (kn, vt):
            ref[2 * n - 1:3 * n - 2] = jnp.zeros((n - 1,) + ref.shape[1:], ref.dtype)
    def turn(ref, dst):
        whole = jnp.concatenate([ref[:, c:c + BLK].T for c in range(0, n * cols, BLK)], axis=0)
        for member in range(n):
            dst[member] = whole[member * cols:(member + 1) * cols]

    def remote(src, dst, ss, rs, dev):
        return pltpu.make_async_remote_copy(src_ref=src, dst_ref=dst, send_sem=ss, recv_sem=rs,
                                            device_id=dev, device_id_type=MESH)

    def exchange(src, dst, ss, rs):
        def send(to):
            remote(src.at[to], dst.at[me], ss, rs.at[mine], device(plane, to)).start()

        def take(pair):
            remote(src.at[pl.ds(0, 2)], dst.at[pl.ds(2 * pair, 2)], ss, rs.at[pair], device(plane, mate)).wait_recv()

        def take_mate():
            remote(src.at[0], dst.at[mate], ss, rs.at[mine], device(plane, mate)).wait_recv()

        def sent():
            part = src.at[pl.ds(0, n - 1)]
            remote(part, part, ss, rs.at[0], device(plane, mate)).wait_send()
        return send, take, take_mate, sent

    k_send, k_take, k_mate, k_sent = exchange(k_src, k_own, send_s.at[0], k_rs)
    q_send, q_take, q_mate, q_sent = exchange(q_src, q_own, send_s.at[1], q_rs)
    v_send, v_take, v_mate, v_sent = exchange(v_src, v_own, send_s.at[2], v_rs)

    def forward(which, halo, member, src):
        pair = member // 2

        @pl.when(jnp.logical_and(has_next, member >= 1))
        def _():
            remote(src, halo.at[member - 1], halo_ss.at[which, 0], halo_rs.at[which, 0, pair],
                   device(plane + 1, me)).start()

        @pl.when(jnp.logical_and(has_prev, member <= n - 2))
        def _():
            remote(src, halo.at[n - 1 + member], halo_ss.at[which, 1], halo_rs.at[which, 1, pair],
                   device(plane - 1, me)).start()

    def landed(which, halo, way, pair, first, count):
        part = halo.at[pl.ds(first, count)]
        remote(part, part, halo_ss.at[which, way], halo_rs.at[which, way, pair], device(plane, mate)).wait_recv()

    def take_halo(which, halo, pair, use):
        @pl.when(jnp.logical_and(has_prev, pair == 0))
        def _():
            landed(which, halo, 0, pair, 0, 1)
            use(0, halo.at[0])

        @pl.when(jnp.logical_and(has_prev, pair > 0))
        def _():
            landed(which, halo, 0, pair, 2 * pair - 1, 2)
            for r in range(2):
                use(2 * pair - 1 + r, halo.at[2 * pair - 1 + r])

        @pl.when(jnp.logical_and(has_next, pair == pairs - 1))
        def _():
            landed(which, halo, 1, pair, 2 * n - 3, 1)
            use(3 * n - 3, halo.at[2 * n - 3])

        @pl.when(jnp.logical_and(has_next, pair < pairs - 1))
        def _():
            landed(which, halo, 1, pair, n - 1 + 2 * pair, 2)
            for r in range(2):
                use(2 * n - 1 + 2 * pair + r, halo.at[n - 1 + 2 * pair + r])

    def sent_up(which, halo):
        part = halo.at[pl.ds(0, n - 1)]
        remote(part, part, halo_ss.at[which, 0], halo_rs.at[which, 0], device(plane, mate)).wait_send()

    def sent_down(which, halo):
        part = halo.at[pl.ds(n - 1, n - 1)]
        remote(part, part, halo_ss.at[which, 1], halo_rs.at[which, 1], device(plane, mate)).wait_send()

    across = grp // 2
    fold_pair, grp_pair = mine // across, mine % across

    def to_pair(step):
        return (fold_pair + step // across) % fold * across + (grp_pair + step % across) % across

    def from_pair(step):
        return (fold_pair + fold - step // across) % fold * across + (grp_pair + across - step % across) % across

    def arrival(turn):
        return turn * across % (pairs - 1) + turn // (pairs - 1) * (pairs - 1)

    def out_order(send):
        for turn in range(1, pairs):
            for r in (1, 0):
                send(2 * to_pair(arrival(turn)) + r)

    loads[0].wait()
    turn(k_in, k_src)
    pl.semaphore_wait(barrier, n - 1 + has_prev.astype(jnp.int32) + has_next.astype(jnp.int32))
    forward(0, k_halo, me, k_src.at[me])
    k_send(mate)
    out_order(k_send)
    loads[2].wait()
    turn(v_in, v_src)
    forward(1, v_halo, me, v_src.at[me])
    v_send(mate)
    loads[1].wait()
    turn(q_in, q_src)
    q_send(mate)
    out_order(v_send)
    keep = pltpu.make_async_copy(q_src.at[me], q_own.at[me], keep_s.at[0])
    keep.start()
    def natural(slot, src):
        kn[slot] = src[...].T

    natural(n - 1 + me, k_src.at[me])
    vt[n - 1 + me] = v_src[me]
    k_mate()
    forward(0, k_halo, mate, k_own.at[mate])
    v_mate()
    forward(1, v_halo, mate, v_own.at[mate])
    natural(n - 1 + mate, k_own.at[mate])
    vt[n - 1 + mate] = v_own[mate]
    def take_k(step, carry):
        pair = from_pair(arrival(step))
        k_take(pair)
        for r in range(2):
            forward(0, k_halo, 2 * pair + r, k_own.at[2 * pair + r])
        for r in range(2):
            natural(n - 1 + 2 * pair + r, k_own.at[2 * pair + r])
        return carry

    lax.fori_loop(1, pairs, take_k, 0)
    out_order(q_send)
    def take_v(step, carry):
        pair = from_pair(arrival(step))
        v_take(pair)
        for r in range(2):
            forward(1, v_halo, 2 * pair + r, v_own.at[2 * pair + r])
        for r in range(2):
            vt[n - 1 + 2 * pair + r] = v_own[2 * pair + r]
        return carry

    lax.fori_loop(1, pairs, take_v, 0)
    def k_far(step, carry):
        take_halo(0, k_halo, from_pair(arrival(step)), natural)
        return carry

    lax.fori_loop(0, pairs, k_far, 0)
    loads[3].wait()
    factor = math.log2(math.e) / math.sqrt(HDIM)
    blocks = img.shape[0]
    base = plane * n

    def span(block):
        own_id = img[block]
        before, after = jnp.int32(0), jnp.int32(0)
        for d in range(1, MOST):
            low = jnp.where(block >= d, img[jnp.maximum(block - d, 0)], -1)
            high = jnp.where(block + d < blocks, img[jnp.minimum(block + d, blocks - 1)], -1)
            before += (low == own_id).astype(jnp.int32)
            after += (high == own_id).astype(jnp.int32)
        return before, before + after + 1

    def first_slot(m):
        before, count = span(base + m)
        return m + n - 1 - before, count

    def weights(m, slot):
        start, count = first_slot(m)
        rows = []
        for h in range(heads):
            q_h = q_own[m, h * HDIM:(h + 1) * HDIM]
            none = jnp.zeros_like(q_h)
            rows.append(jnp.concatenate([q_h if j == h else none for j in range(heads)], axis=1))
        q_all = jnp.concatenate(rows, axis=0)
        top = jnp.full((1, heads * BLK), NEG, jnp.float32)
        for t in range(MOST):
            s = jnp.dot(kn[start + t], q_all, preferred_element_type=jnp.float32)
            s_scr[slot, t] = s
            top = jnp.maximum(top, jnp.where(t < count, jnp.max(s, axis=0, keepdims=True), NEG))
        total = jnp.zeros((8, heads * BLK), jnp.float32)
        for t in range(MOST):
            shift = jnp.where(t < count, -top * factor, NEG)
            w = jnp.exp2(s_scr[slot, t] * factor + shift)
            total = total + jnp.sum(w.reshape(BLK // 8, 8, heads * BLK), axis=0)
            p_scr[m, t * BLK:(t + 1) * BLK] = w.astype(jnp.bfloat16)
        l_scr[m] = jnp.sum(total, axis=0, keepdims=True)

    def score(pair):
        for r in range(2):
            weights(2 * pair + r, r)

    def score_step(step, carry):
        pair = from_pair(arrival(step))

        @pl.when(step == 0)
        def _():
            keep.wait()
            q_mate()

        @pl.when(step > 0)
        def _():
            q_take(pair)
        score(pair)
        return carry

    lax.fori_loop(0, pairs, score_step, 0)
    def hold(slot, src):
        vt[slot] = src[...]

    def v_far(step, carry):
        take_halo(1, v_halo, from_pair(arrival(step)), hold)
        return carry

    lax.fori_loop(0, pairs, v_far, 0)
    o_send, o_take, o_mate, o_sent = exchange(o_src, o_own, send_s.at[3], o_rs)

    def finish(step, carry):
        pair = to_pair(pairs - 1 - step)
        for r in range(2):
            m = 2 * pair + r
            start, _ = first_slot(m)
            v = jnp.concatenate([vt[start + t] for t in range(MOST)], axis=1)
            res = jnp.dot(v, p_scr[m], preferred_element_type=jnp.float32)
            res = jnp.concatenate([res[h * HDIM:(h + 1) * HDIM, h * BLK:(h + 1) * BLK]
                                   / l_scr[m, :, h * BLK:(h + 1) * BLK] for h in range(heads)], axis=0)
            o_src[m] = res.astype(jnp.bfloat16)
        for r in range(2):
            m = 2 * pair + r

            @pl.when(m != me)
            def _():
                o_send(m)
        return carry

    lax.fori_loop(0, pairs, finish, 0)
    o_own[me] = o_src[me]
    k_sent()
    q_sent()
    v_sent()
    for which, halo in ((0, k_halo), (1, v_halo)):
        @pl.when(has_next)
        def _():
            sent_up(which, halo)

        @pl.when(has_prev)
        def _():
            sent_down(which, halo)
    o_mate()
    for step in range(1, pairs):
        o_take(from_pair(step))
    flat = jnp.concatenate([o_own[member] for member in range(n)], axis=0)
    for c in range(0, n * cols, BLK):
        out[:, c:c + BLK] = flat[c:c + BLK].T
    o_sent()


def solution(mesh):
    wide, grp = mesh.shape["wide"], mesh.shape["grp"]
    fold = MOST // grp
    n = fold * grp
    planes = wide // fold

    def body(query_rows, key_rows, value_rows, block_image):
        rows, width = query_rows.shape
        heads = width // HDIM // n
        cols = heads * HDIM
        bf, f32 = jnp.bfloat16, jnp.float32
        hbm = pl.BlockSpec(memory_space=pltpu.HBM)
        dma = pltpu.SemaphoreType.DMA
        slices = pltpu.VMEM((n, cols, BLK), bf)
        halo = pltpu.VMEM((2 * n - 2, cols, BLK), bf)
        lanes = heads * BLK
        args = [pltpu.with_memory_space_constraint(a, pltpu.HBM)
                for a in (block_image, query_rows, key_rows, value_rows)]
        return pl.pallas_call(
            functools.partial(kernel, (planes, fold, grp, heads)),
            out_shape=jax.ShapeDtypeStruct((rows, width), bf),
            in_specs=[hbm] * 4,
            out_specs=pl.BlockSpec(memory_space=pltpu.VMEM),
            scratch_shapes=[pltpu.SMEM(block_image.shape, jnp.int32)]
            + [pltpu.VMEM((rows, width), bf)] * 3 + [slices] * 6 + [halo] * 2 + [
                pltpu.VMEM((3 * n - 2, BLK, cols), bf),
                pltpu.VMEM((3 * n - 2, cols, BLK), bf),
                pltpu.VMEM((n, 1, lanes), f32),
                pltpu.VMEM((2, MOST, BLK, lanes), f32),
                pltpu.VMEM((n, MOST * BLK, lanes), bf),
                slices, slices,
            ] + [dma((4,))] + [dma((n // 2,))] * 4 + [dma((4,)), dma((2, 2)), dma((2, 2, n // 2)), dma((1,))],
            compiler_params=pltpu.CompilerParams(collective_id=0, has_side_effects=True,
                                                 vmem_limit_bytes=40 << 20),
        )(*args)

    return jax.shard_map(
        body,
        mesh=mesh,
        in_specs=(
            P(("wide", "grp"), None),
            P(("wide", "grp"), None),
            P(("wide", "grp"), None),
            P(),
        ),
        out_specs=P(("wide", "grp"), None),
        check_vma=False,
    )
```

```python
import functools
import math

import jax
import jax.numpy as jnp
from jax import lax
from jax.experimental import pallas as pl
from jax.experimental.pallas import tpu as pltpu
from jax.sharding import PartitionSpec as P

HDIM = 80
BLK = 128
MOST = 8
NEG = -1e30
MESH = pl.DeviceIdType.MESH


def kernel(cfg, img_hbm, q_hbm, k_hbm, v_hbm, out, img, q_in, k_in, v_in, k_src, q_src, v_src,
           k_own, q_own, v_own, k_halo, v_halo, kn, vt, l_scr, s_scr, p_scr, start_scr, count_scr, o_src, o_own,
           load_s, k_rs, q_rs, v_rs, o_rs, send_s, halo_ss, halo_rs, keep_s):
    planes, fold, grp, heads = cfg
    n = fold * grp
    cols = heads * HDIM
    pairs = n // 2
    wide_at, grp_at = lax.axis_index("wide"), lax.axis_index("grp")
    plane = wide_at // fold
    fold_at = wide_at % fold
    me = fold_at * grp + grp_at
    mine = me // 2
    mate = mine * 2 + 1 - me % 2
    has_prev, has_next = plane > 0, plane < planes - 1

    loads = [pltpu.make_async_copy(src, dst, load_s.at[i])
             for i, (src, dst) in enumerate(((k_hbm, k_in), (q_hbm, q_in), (v_hbm, v_in), (img_hbm, img)))]
    for load in loads:
        load.start()
    def device(at_plane, member):
        return (at_plane * fold + member // grp, member % grp)

    barrier = pltpu.get_barrier_semaphore()
    for i in range(1, n):
        pl.semaphore_signal(barrier, inc=1, device_id=device(plane, (me + i) % n), device_id_type=MESH)

    @pl.when(has_prev)
    def _():
        pl.semaphore_signal(barrier, inc=1, device_id=device(plane - 1, me), device_id_type=MESH)

    @pl.when(has_next)
    def _():
        pl.semaphore_signal(barrier, inc=1, device_id=device(plane + 1, me), device_id_type=MESH)
    def turn(ref, dst):
        whole = jnp.concatenate([ref[:, c:c + BLK].T for c in range(0, n * cols, BLK)], axis=0)
        for member in range(n):
            dst[member] = whole[member * cols:(member + 1) * cols]

    def remote(src, dst, ss, rs, dev):
        return pltpu.make_async_remote_copy(src_ref=src, dst_ref=dst, send_sem=ss, recv_sem=rs,
                                            device_id=dev, device_id_type=MESH)

    def exchange(src, dst, ss, rs):
        def send(to):
            remote(src.at[to], dst.at[me], ss, rs.at[mine], device(plane, to)).start()

        def take(pair):
            remote(src.at[pl.ds(0, 2)], dst.at[pl.ds(2 * pair, 2)], ss, rs.at[pair], device(plane, mate)).wait_recv()

        def take_mate():
            remote(src.at[0], dst.at[mate], ss, rs.at[mine], device(plane, mate)).wait_recv()

        def sent():
            part = src.at[pl.ds(0, n - 1)]
            remote(part, part, ss, rs.at[0], device(plane, mate)).wait_send()
        return send, take, take_mate, sent

    k_send, k_take, k_mate, k_sent = exchange(k_src, k_own, send_s.at[0], k_rs)
    q_send, q_take, q_mate, q_sent = exchange(q_src, q_own, send_s.at[1], q_rs)
    v_send, v_take, v_mate, v_sent = exchange(v_src, v_own, send_s.at[2], v_rs)

    def forward(which, halo, member, src, down_first=False):
        pair = member // 2

        def up():
            @pl.when(jnp.logical_and(has_next, member >= 1))
            def _():
                remote(src, halo.at[member - 1], halo_ss.at[which, 0], halo_rs.at[which, 0, pair],
                       device(plane + 1, me)).start()

        def down():
            @pl.when(jnp.logical_and(has_prev, member <= n - 2))
            def _():
                remote(src, halo.at[n - 1 + member], halo_ss.at[which, 1], halo_rs.at[which, 1, pair],
                       device(plane - 1, me)).start()

        for way in (down, up) if down_first else (up, down):
            way()

    def landed(which, halo, way, pair, first, count):
        part = halo.at[pl.ds(first, count)]
        remote(part, part, halo_ss.at[which, way], halo_rs.at[which, way, pair], device(plane, mate)).wait_recv()

    def take_below(which, halo, pair, use):
        @pl.when(jnp.logical_and(has_prev, pair == 0))
        def _():
            landed(which, halo, 0, pair, 0, 1)
            use(0, halo.at[0])

        @pl.when(jnp.logical_and(has_prev, pair > 0))
        def _():
            landed(which, halo, 0, pair, 2 * pair - 1, 2)
            for r in range(2):
                use(2 * pair - 1 + r, halo.at[2 * pair - 1 + r])

    def take_above(which, halo, pair, use):
        @pl.when(jnp.logical_and(has_next, pair == pairs - 1))
        def _():
            landed(which, halo, 1, pair, 2 * n - 3, 1)
            use(3 * n - 3, halo.at[2 * n - 3])

        @pl.when(jnp.logical_and(has_next, pair < pairs - 1))
        def _():
            landed(which, halo, 1, pair, n - 1 + 2 * pair, 2)
            for r in range(2):
                use(2 * n - 1 + 2 * pair + r, halo.at[n - 1 + 2 * pair + r])

    def sent_up(which, halo):
        part = halo.at[pl.ds(0, n - 1)]
        remote(part, part, halo_ss.at[which, 0], halo_rs.at[which, 0], device(plane, mate)).wait_send()

    def sent_down(which, halo):
        part = halo.at[pl.ds(n - 1, n - 1)]
        remote(part, part, halo_ss.at[which, 1], halo_rs.at[which, 1], device(plane, mate)).wait_send()

    across = grp // 2
    fold_pair, grp_pair = mine // across, mine % across

    def to_pair(step):
        return (fold_pair + step // across) % fold * across + (grp_pair + step % across) % across

    def from_pair(step):
        return (fold_pair + fold - step // across) % fold * across + (grp_pair + across - step % across) % across

    def arrival(turn):
        return turn * across % (pairs - 1) + turn // (pairs - 1) * (pairs - 1)

    first_step = (fold - fold_pair) % fold * across + (across - grp_pair) % across

    def turn_order(turn):
        step = arrival(turn)
        other = jnp.where(step == 1, pairs - 1, jnp.where(step == pairs - 1, 1, step))
        return jnp.where(first_step == pairs - 1, other, step)

    def out_order(send):
        for turn in range(1, pairs):
            for r in (1, 0):
                send(2 * to_pair(arrival(turn)) + r)

    loads[0].wait()
    turn(k_in, k_src)
    pl.semaphore_wait(barrier, n - 1 + has_prev.astype(jnp.int32) + has_next.astype(jnp.int32))
    forward(0, k_halo, me, k_src.at[me])
    k_send(mate)
    out_order(k_send)
    loads[2].wait()
    turn(v_in, v_src)
    forward(1, v_halo, me, v_src.at[me], True)
    v_send(mate)
    loads[1].wait()
    turn(q_in, q_src)
    q_send(mate)
    out_order(v_send)
    keep = pltpu.make_async_copy(q_src.at[me], q_own.at[me], keep_s.at[0])
    keep.start()
    def natural(slot, src):
        kn[slot] = src[...].T

    loads[3].wait()
    factor = math.log2(math.e) / math.sqrt(HDIM)
    blocks = img.shape[0]
    base = plane * n

    def span(block):
        own_id = img[block]
        before, after = jnp.int32(0), jnp.int32(0)
        for d in range(1, MOST):
            low = jnp.where(block >= d, img[jnp.maximum(block - d, 0)], -1)
            high = jnp.where(block + d < blocks, img[jnp.minimum(block + d, blocks - 1)], -1)
            before += (low == own_id).astype(jnp.int32)
            after += (high == own_id).astype(jnp.int32)
        return before, before + after + 1

    def note_span(m, carry):
        before, count = span(base + m)
        start_scr[m] = m + n - 1 - before
        count_scr[m] = count
        return carry

    lax.fori_loop(0, n, note_span, 0)
    natural(n - 1 + me, k_src.at[me])
    vt[n - 1 + me] = v_src[me]
    k_mate()
    forward(0, k_halo, mate, k_own.at[mate])
    v_mate()
    forward(1, v_halo, mate, v_own.at[mate], True)
    natural(n - 1 + mate, k_own.at[mate])
    vt[n - 1 + mate] = v_own[mate]
    def take_k(step, carry):
        pair = from_pair(arrival(step))
        k_take(pair)
        for r in range(2):
            forward(0, k_halo, 2 * pair + r, k_own.at[2 * pair + r], r == 1)
        for r in range(2):
            natural(n - 1 + 2 * pair + r, k_own.at[2 * pair + r])
        return carry

    lax.fori_loop(1, pairs, take_k, 0)
    out_order(q_send)
    def take_v(step, carry):
        pair = from_pair(turn_order(step))
        v_take(pair)
        for r in range(2):
            forward(1, v_halo, 2 * pair + r, v_own.at[2 * pair + r], r == 1)
        for r in range(2):
            vt[n - 1 + 2 * pair + r] = v_own[2 * pair + r]
        return carry

    lax.fori_loop(1, pairs, take_v, 0)
    def k_far(step, carry):
        take_below(0, k_halo, from_pair(arrival(step)), natural)
        take_above(0, k_halo, from_pair(arrival(step)), natural)
        return carry

    lax.fori_loop(0, pairs, k_far, 0)
    def scores(m, s_ref):
        start, count = start_scr[m], count_scr[m]
        rows = []
        for h in range(heads):
            q_h = q_own[m, h * HDIM:(h + 1) * HDIM]
            none = jnp.zeros_like(q_h)
            rows.append(jnp.concatenate([q_h if j == h else none for j in range(heads)], axis=1))
        q_all = jnp.concatenate(rows, axis=0)
        top = jnp.full((8, heads * BLK), NEG, jnp.float32)
        for t in range(MOST):
            s = jnp.dot(kn[start + jnp.where(t < count, t, 0)], q_all, preferred_element_type=jnp.float32)
            s_ref[t] = s
            high = jnp.max(s.reshape(BLK // 8, 8, heads * BLK), axis=0)
            top = jnp.maximum(top, jnp.where(t < count, high, NEG))
        return jnp.max(top, axis=0, keepdims=True), count

    def weigh(m, s_ref, top, count):
        total = jnp.zeros((8, heads * BLK), jnp.float32)
        for t in range(MOST):
            shift = jnp.where(t < count, -top * factor, NEG)
            w = jnp.exp2(s_ref[t] * factor + shift)
            total = total + jnp.sum(w.reshape(BLK // 8, 8, heads * BLK), axis=0)
            p_scr[m, t * BLK:(t + 1) * BLK] = w.astype(jnp.bfloat16)
        l_scr[m] = jnp.sum(total, axis=0, keepdims=True)

    def hold(slot, src):
        vt[slot] = src[...]

    o_send, o_take, o_mate, o_sent = exchange(o_src, o_own, send_s.at[3], o_rs)

    def finish(pair):
        for r in range(2):
            m = 2 * pair + r
            start, count = start_scr[m], count_scr[m]
            v = jnp.concatenate([vt[start + jnp.where(t < count, t, 0)] for t in range(MOST)], axis=1)
            res = jnp.dot(v, p_scr[m], preferred_element_type=jnp.float32)
            res = jnp.concatenate([res[h * HDIM:(h + 1) * HDIM, h * BLK:(h + 1) * BLK]
                                   / l_scr[m, :, h * BLK:(h + 1) * BLK] for h in range(heads)], axis=0)
            o_src[m] = res.astype(jnp.bfloat16)
        for r in range(2):
            m = 2 * pair + r

            @pl.when(m != me)
            def _():
                o_send(m)

    keep.wait()
    q_mate()
    pair = from_pair(0)
    now = scores(2 * pair, s_scr.at[0])
    for step in range(pairs):
        if step < pairs - 1:
            coming = from_pair(turn_order(step + 1))
            q_take(coming)
        later = scores(2 * pair + 1, s_scr.at[1])
        weigh(2 * pair, s_scr.at[0], *now)
        if step < pairs - 1:
            now = scores(2 * coming, s_scr.at[0])
        weigh(2 * pair + 1, s_scr.at[1], *later)
        pair = coming
        if step == pairs - 2:
            @pl.when(jnp.logical_not(has_prev))
            def _():
                take_above(1, v_halo, 0, hold)

                @pl.when(mine != 0)
                def _():
                    finish(0)
    @pl.when(has_prev)
    def _():
        for pair in range(pairs):
            take_below(1, v_halo, pair, hold)
        take_above(1, v_halo, 0, hold)

        @pl.when(mine != 0)
        def _():
            finish(0)

    def leave(pair, carry):
        take_above(1, v_halo, pair, hold)

        @pl.when(pair != mine)
        def _():
            finish(pair)
        return carry

    lax.fori_loop(1, pairs, leave, 0)
    finish(mine)
    o_own[me] = o_src[me]
    k_sent()
    q_sent()
    v_sent()
    for which, halo in ((0, k_halo), (1, v_halo)):
        @pl.when(has_next)
        def _():
            sent_up(which, halo)

        @pl.when(has_prev)
        def _():
            sent_down(which, halo)
    o_mate()
    for step in range(1, pairs):
        o_take(from_pair(step))
    flat = jnp.concatenate([o_own[member] for member in range(n)], axis=0)
    for c in range(0, n * cols, BLK):
        out[:, c:c + BLK] = flat[c:c + BLK].T
    o_sent()


def solution(mesh):
    wide, grp = mesh.shape["wide"], mesh.shape["grp"]
    fold = MOST // grp
    n = fold * grp
    planes = wide // fold

    def body(query_rows, key_rows, value_rows, block_image):
        rows, width = query_rows.shape
        heads = width // HDIM // n
        cols = heads * HDIM
        bf, f32 = jnp.bfloat16, jnp.float32
        hbm = pl.BlockSpec(memory_space=pltpu.HBM)
        dma = pltpu.SemaphoreType.DMA
        slices = pltpu.VMEM((n, cols, BLK), bf)
        halo = pltpu.VMEM((2 * n - 2, cols, BLK), bf)
        lanes = heads * BLK
        args = [pltpu.with_memory_space_constraint(a, pltpu.HBM)
                for a in (block_image, query_rows, key_rows, value_rows)]
        return pl.pallas_call(
            functools.partial(kernel, (planes, fold, grp, heads)),
            out_shape=jax.ShapeDtypeStruct((rows, width), bf),
            in_specs=[hbm] * 4,
            out_specs=pl.BlockSpec(memory_space=pltpu.VMEM),
            scratch_shapes=[pltpu.SMEM(block_image.shape, jnp.int32)]
            + [pltpu.VMEM((rows, width), bf)] * 3 + [slices] * 6 + [halo] * 2 + [
                pltpu.VMEM((3 * n - 2, BLK, cols), bf),
                pltpu.VMEM((3 * n - 2, cols, BLK), bf),
                pltpu.VMEM((n, 1, lanes), f32),
                pltpu.VMEM((4, MOST, BLK, lanes), f32),
                pltpu.VMEM((n, MOST * BLK, lanes), bf),
                pltpu.SMEM((n,), jnp.int32), pltpu.SMEM((n,), jnp.int32),
                slices, slices,
            ] + [dma((4,))] + [dma((n // 2,))] * 4 + [dma((4,)), dma((2, 2)), dma((2, 2, n // 2)), dma((1,))],
            compiler_params=pltpu.CompilerParams(collective_id=0, has_side_effects=True,
                                                 vmem_limit_bytes=40 << 20),
        )(*args)

    return jax.shard_map(
        body,
        mesh=mesh,
        in_specs=(
            P(("wide", "grp"), None),
            P(("wide", "grp"), None),
            P(("wide", "grp"), None),
            P(),
        ),
        out_specs=P(("wide", "grp"), None),
        check_vma=False,
    )
```

```python
import functools
import math

import jax
import jax.numpy as jnp
from jax import lax
from jax.experimental import pallas as pl
from jax.experimental.pallas import tpu as pltpu
from jax.sharding import PartitionSpec as P

HDIM = 80
BLK = 128
MOST = 8
NEG = -1e30
MESH = pl.DeviceIdType.MESH


def kernel(cfg, img_hbm, q_hbm, k_hbm, v_hbm, out, img, q_in, k_in, v_in, k_src, q_src, v_src,
           k_own, q_own, v_own, k_halo, v_halo, kn, vt, l_scr, s_scr, p_scr, start_scr, count_scr, o_src, o_own,
           load_s, k_rs, q_rs, v_rs, o_rs, send_s, halo_ss, halo_rs):
    planes, fold, grp, heads = cfg
    n = fold * grp
    cols = heads * HDIM
    pairs = n // 2
    wide_at, grp_at = lax.axis_index("wide"), lax.axis_index("grp")
    plane = wide_at // fold
    fold_at = wide_at % fold
    me = fold_at * grp + grp_at
    mine = me // 2
    mate = mine * 2 + 1 - me % 2
    has_prev, has_next = plane > 0, plane < planes - 1

    loads = [pltpu.make_async_copy(src, dst, load_s.at[i])
             for i, (src, dst) in enumerate(((k_hbm, k_in), (q_hbm, q_in), (v_hbm, v_in), (img_hbm, img)))]
    for load in loads:
        load.start()
    def device(at_plane, member):
        return (at_plane * fold + member // grp, member % grp)

    barrier = pltpu.get_barrier_semaphore()
    for i in range(1, n):
        pl.semaphore_signal(barrier, inc=1, device_id=device(plane, (me + i) % n), device_id_type=MESH)

    @pl.when(has_prev)
    def _():
        pl.semaphore_signal(barrier, inc=1, device_id=device(plane - 1, me), device_id_type=MESH)

    @pl.when(has_next)
    def _():
        pl.semaphore_signal(barrier, inc=1, device_id=device(plane + 1, me), device_id_type=MESH)
    def turn(ref, dst):
        whole = jnp.concatenate([ref[:, c:c + BLK].T for c in range(0, n * cols, BLK)], axis=0)
        for member in range(n):
            dst[member] = whole[member * cols:(member + 1) * cols]

    def remote(src, dst, ss, rs, dev):
        return pltpu.make_async_remote_copy(src_ref=src, dst_ref=dst, send_sem=ss, recv_sem=rs,
                                            device_id=dev, device_id_type=MESH)

    def exchange(src, dst, ss, rs):
        def send(to):
            remote(src.at[to], dst.at[me], ss, rs.at[mine % rs.shape[0]], device(plane, to)).start()

        def take(pair):
            remote(src.at[pl.ds(0, 2)], dst.at[pl.ds(2 * pair, 2)], ss, rs.at[pair], device(plane, mate)).wait_recv()

        def take_mate():
            remote(src.at[0], dst.at[mate], ss, rs.at[mine], device(plane, mate)).wait_recv()

        def take_all():
            part = src.at[pl.ds(0, n - 1)]
            remote(part, part, ss, rs.at[0], device(plane, mate)).wait_recv()

        def sent():
            part = src.at[pl.ds(0, n - 1)]
            remote(part, part, ss, rs.at[0], device(plane, mate)).wait_send()
        return send, take, take_mate, take_all, sent

    k_send, k_take, k_mate, _, _ = exchange(k_src, k_own, send_s.at[0], k_rs)
    q_send, q_take, q_mate, _, _ = exchange(q_src, q_own, send_s.at[0], q_rs)
    v_send, v_take, v_mate, _, _ = exchange(v_src, v_own, send_s.at[0], v_rs)

    def forward(which, halo, member, src, down_first=False):
        pair = member // 2

        def up():
            @pl.when(jnp.logical_and(has_next, member >= 1))
            def _():
                remote(src, halo.at[member - 1], halo_ss.at[which, 0], halo_rs.at[which, 0, pair],
                       device(plane + 1, me)).start()

        def down():
            @pl.when(jnp.logical_and(has_prev, member <= n - 2))
            def _():
                remote(src, halo.at[n - 1 + member], halo_ss.at[which, 1], halo_rs.at[which, 1, pair],
                       device(plane - 1, me)).start()

        for way in (down, up) if down_first else (up, down):
            way()

    def forward_pair(which, halo, pair, src):
        def up(first, count):
            remote(src.at[pl.ds(first, count)], halo.at[pl.ds(first - 1, count)], halo_ss.at[which, 0],
                   halo_rs.at[which, 0, pair], device(plane + 1, me)).start()

        def down(first, count):
            remote(src.at[pl.ds(first, count)], halo.at[pl.ds(n - 1 + first, count)], halo_ss.at[which, 1],
                   halo_rs.at[which, 1, pair], device(plane - 1, me)).start()

        @pl.when(jnp.logical_and(has_next, pair > 0))
        def _():
            up(2 * pair, 2)

        @pl.when(jnp.logical_and(has_next, pair == 0))
        def _():
            up(1, 1)

        @pl.when(jnp.logical_and(has_prev, pair < pairs - 1))
        def _():
            down(2 * pair, 2)

        @pl.when(jnp.logical_and(has_prev, pair == pairs - 1))
        def _():
            down(n - 2, 1)

    def landed(which, halo, way, pair, first, count):
        part = halo.at[pl.ds(first, count)]
        remote(part, part, halo_ss.at[which, way], halo_rs.at[which, way, pair], device(plane, mate)).wait_recv()

    def take_below(which, halo, pair, use):
        @pl.when(jnp.logical_and(has_prev, pair == 0))
        def _():
            landed(which, halo, 0, pair, 0, 1)
            use(0, halo.at[0])

        @pl.when(jnp.logical_and(has_prev, pair > 0))
        def _():
            landed(which, halo, 0, pair, 2 * pair - 1, 2)
            for r in range(2):
                use(2 * pair - 1 + r, halo.at[2 * pair - 1 + r])

    def take_above(which, halo, pair, use):
        @pl.when(jnp.logical_and(has_next, pair == pairs - 1))
        def _():
            landed(which, halo, 1, pair, 2 * n - 3, 1)
            use(3 * n - 3, halo.at[2 * n - 3])

        @pl.when(jnp.logical_and(has_next, pair < pairs - 1))
        def _():
            landed(which, halo, 1, pair, n - 1 + 2 * pair, 2)
            for r in range(2):
                use(2 * n - 1 + 2 * pair + r, halo.at[n - 1 + 2 * pair + r])

    def sent_up(which, halo):
        part = halo.at[pl.ds(0, n - 1)]
        remote(part, part, halo_ss.at[which, 0], halo_rs.at[which, 0], device(plane, mate)).wait_send()

    def sent_down(which, halo):
        part = halo.at[pl.ds(n - 1, n - 1)]
        remote(part, part, halo_ss.at[which, 1], halo_rs.at[which, 1], device(plane, mate)).wait_send()

    across = grp // 2
    fold_pair, grp_pair = mine // across, mine % across

    def to_pair(step):
        return (fold_pair + step // across) % fold * across + (grp_pair + step % across) % across

    def from_pair(step):
        return (fold_pair + fold - step // across) % fold * across + (grp_pair + across - step % across) % across

    def arrival(turn):
        return turn * across % (pairs - 1) + turn // (pairs - 1) * (pairs - 1)

    first_step = (fold - fold_pair) % fold * across + (across - grp_pair) % across

    def turn_order(turn):
        step = arrival(turn)
        other = jnp.where(step == 1, pairs - 1, jnp.where(step == pairs - 1, 1, step))
        return jnp.where(first_step == pairs - 1, other, step)

    def out_order(send):
        for turn in range(1, pairs):
            for r in (1, 0):
                send(2 * to_pair(arrival(turn)) + r)

    loads[0].wait()
    turn(k_in, k_src)
    pl.semaphore_wait(barrier, n - 1 + has_prev.astype(jnp.int32) + has_next.astype(jnp.int32))
    forward(0, k_halo, me, k_src.at[me])
    k_send(mate)
    out_order(k_send)
    loads[2].wait()
    turn(v_in, v_src)
    forward(1, v_halo, me, v_src.at[me], True)
    v_send(mate)
    loads[1].wait()
    turn(q_in, q_src)
    q_send(mate)
    out_order(v_send)
    def natural(slot, src):
        kn[slot] = src[...].T

    loads[3].wait()
    factor = math.log2(math.e) / math.sqrt(HDIM)
    blocks = img.shape[0]
    base = plane * n

    def span(block):
        own_id = img[block]
        before, after = jnp.int32(0), jnp.int32(0)
        for d in range(1, MOST):
            low = jnp.where(block >= d, img[jnp.maximum(block - d, 0)], -1)
            high = jnp.where(block + d < blocks, img[jnp.minimum(block + d, blocks - 1)], -1)
            before += (low == own_id).astype(jnp.int32)
            after += (high == own_id).astype(jnp.int32)
        return before, before + after + 1

    def note_span(m, carry):
        before, count = span(base + m)
        start_scr[m] = m + n - 1 - before
        count_scr[m] = count
        return carry

    lax.fori_loop(0, n, note_span, 0)
    natural(n - 1 + me, k_src.at[me])
    vt[n - 1 + me] = v_src[me]
    k_mate()
    forward(0, k_halo, mate, k_own.at[mate])
    v_mate()
    forward(1, v_halo, mate, v_own.at[mate], True)
    natural(n - 1 + mate, k_own.at[mate])
    vt[n - 1 + mate] = v_own[mate]
    def take_k(step, carry):
        pair = from_pair(arrival(step))
        k_take(pair)
        forward_pair(0, k_halo, pair, k_own)
        for r in range(2):
            natural(n - 1 + 2 * pair + r, k_own.at[2 * pair + r])
        return carry

    lax.fori_loop(1, pairs, take_k, 0)
    out_order(q_send)
    def take_v(step, carry):
        pair = from_pair(turn_order(step))
        v_take(pair)
        forward_pair(1, v_halo, pair, v_own)
        for r in range(2):
            vt[n - 1 + 2 * pair + r] = v_own[2 * pair + r]
        return carry

    lax.fori_loop(1, pairs, take_v, 0)
    def k_far(step, carry):
        take_below(0, k_halo, from_pair(arrival(step)), natural)
        take_above(0, k_halo, from_pair(arrival(step)), natural)
        return carry

    lax.fori_loop(0, pairs, k_far, 0)
    def scores(m, s_ref):
        start, count = start_scr[m], count_scr[m]
        rows = []
        for h in range(heads):
            q_h = q_own[m, h * HDIM:(h + 1) * HDIM]
            none = jnp.zeros_like(q_h)
            rows.append(jnp.concatenate([q_h if j == h else none for j in range(heads)], axis=1))
        q_all = jnp.concatenate(rows, axis=0)
        top = jnp.full((8, heads * BLK), NEG, jnp.float32)
        for t in range(MOST):
            s = jnp.dot(kn[start + jnp.where(t < count, t, 0)], q_all, preferred_element_type=jnp.float32)
            s_ref[t] = s
            high = jnp.max(s.reshape(BLK // 8, 8, heads * BLK), axis=0)
            top = jnp.maximum(top, jnp.where(t < count, high, NEG))
        return jnp.max(top, axis=0, keepdims=True), count

    def weigh(m, s_ref, top, count):
        total = jnp.zeros((8, heads * BLK), jnp.float32)
        for t in range(MOST):
            shift = jnp.where(t < count, -top * factor, NEG)
            w = jnp.exp2(s_ref[t] * factor + shift)
            total = total + jnp.sum(w.reshape(BLK // 8, 8, heads * BLK), axis=0)
            p_scr[m, t * BLK:(t + 1) * BLK] = w.astype(jnp.bfloat16)
        l_scr[m] = jnp.sum(total, axis=0, keepdims=True)

    def hold(slot, src):
        vt[slot] = src[...]

    o_send, _, _, o_take, o_sent = exchange(o_src, o_own, send_s.at[1], o_rs)

    def finish(pair):
        for r in range(2):
            m = 2 * pair + r
            start, count = start_scr[m], count_scr[m]
            v = jnp.concatenate([vt[start + jnp.where(t < count, t, 0)] for t in range(MOST)], axis=1)
            res = jnp.dot(v, p_scr[m], preferred_element_type=jnp.float32)
            res = jnp.concatenate([res[h * HDIM:(h + 1) * HDIM, h * BLK:(h + 1) * BLK]
                                   / l_scr[m, :, h * BLK:(h + 1) * BLK] for h in range(heads)], axis=0)
            o_src[m] = res.astype(jnp.bfloat16)
        for r in range(2):
            m = 2 * pair + r

            @pl.when(m != me)
            def _():
                o_send(m)

    q_own[me] = q_src[me]
    q_mate()
    pair = from_pair(0)
    now = scores(2 * pair, s_scr.at[0])
    for step in range(pairs):
        if step < pairs - 1:
            coming = from_pair(turn_order(step + 1))
            q_take(coming)
        later = scores(2 * pair + 1, s_scr.at[1])
        weigh(2 * pair, s_scr.at[0], *now)
        if step < pairs - 1:
            now = scores(2 * coming, s_scr.at[0])
        weigh(2 * pair + 1, s_scr.at[1], *later)
        pair = coming
        if step == pairs - 2:
            @pl.when(jnp.logical_not(has_prev))
            def _():
                take_above(1, v_halo, 0, hold)

                @pl.when(mine != 0)
                def _():
                    finish(0)
    @pl.when(has_prev)
    def _():
        for pair in range(pairs):
            take_below(1, v_halo, pair, hold)
        take_above(1, v_halo, 0, hold)

        @pl.when(mine != 0)
        def _():
            finish(0)

    def leave(pair, carry):
        take_above(1, v_halo, pair, hold)

        @pl.when(pair != mine)
        def _():
            finish(pair)
        return carry

    lax.fori_loop(1, pairs, leave, 0)
    finish(mine)
    o_own[me] = o_src[me]
    part = vt.at[pl.ds(0, 3 * n - 3)]
    remote(part, part, send_s.at[0], k_rs.at[0], device(plane, mate)).wait_send()
    for which, halo in ((0, k_halo), (1, v_halo)):
        @pl.when(has_next)
        def _():
            sent_up(which, halo)

        @pl.when(has_prev)
        def _():
            sent_down(which, halo)
    o_take()
    flat = jnp.concatenate([o_own[member] for member in range(n)], axis=0)
    for c in range(0, n * cols, BLK):
        out[:, c:c + BLK] = flat[c:c + BLK].T
    o_sent()


def solution(mesh):
    wide, grp = mesh.shape["wide"], mesh.shape["grp"]
    fold = MOST // grp
    n = fold * grp
    planes = wide // fold

    def body(query_rows, key_rows, value_rows, block_image):
        rows, width = query_rows.shape
        heads = width // HDIM // n
        cols = heads * HDIM
        bf, f32 = jnp.bfloat16, jnp.float32
        hbm = pl.BlockSpec(memory_space=pltpu.HBM)
        dma = pltpu.SemaphoreType.DMA
        slices = pltpu.VMEM((n, cols, BLK), bf)
        halo = pltpu.VMEM((2 * n - 2, cols, BLK), bf)
        lanes = heads * BLK
        args = [pltpu.with_memory_space_constraint(a, pltpu.HBM)
                for a in (block_image, query_rows, key_rows, value_rows)]
        return pl.pallas_call(
            functools.partial(kernel, (planes, fold, grp, heads)),
            out_shape=jax.ShapeDtypeStruct((rows, width), bf),
            in_specs=[hbm] * 4,
            out_specs=pl.BlockSpec(memory_space=pltpu.VMEM),
            scratch_shapes=[pltpu.SMEM(block_image.shape, jnp.int32)]
            + [pltpu.VMEM((rows, width), bf)] * 3 + [slices] * 6 + [halo] * 2 + [
                pltpu.VMEM((3 * n - 2, BLK, cols), bf),
                pltpu.VMEM((3 * n - 2, cols, BLK), bf),
                pltpu.VMEM((n, 1, lanes), f32),
                pltpu.VMEM((4, MOST, BLK, lanes), f32),
                pltpu.VMEM((n, MOST * BLK, lanes), bf),
                pltpu.SMEM((n,), jnp.int32), pltpu.SMEM((n,), jnp.int32),
                slices, slices,
            ] + [dma((4,))] + [dma((n // 2,))] * 3 + [dma((1,)), dma((2,)), dma((2, 2)), dma((2, 2, n // 2))],
            compiler_params=pltpu.CompilerParams(collective_id=0, has_side_effects=True,
                                                 vmem_limit_bytes=40 << 20),
        )(*args)

    return jax.shard_map(
        body,
        mesh=mesh,
        in_specs=(
            P(("wide", "grp"), None),
            P(("wide", "grp"), None),
            P(("wide", "grp"), None),
            P(),
        ),
        out_specs=P(("wide", "grp"), None),
        check_vma=False,
    )
```

```python
import functools
import math

import jax
import jax.numpy as jnp
from jax import lax
from jax.experimental import pallas as pl
from jax.experimental.pallas import tpu as pltpu
from jax.sharding import PartitionSpec as P

HDIM = 80
BLK = 128
MOST = 8
NEG = -1e30
MESH = pl.DeviceIdType.MESH


def kernel(cfg, img_hbm, q_hbm, k_hbm, v_hbm, out, img, q_in, k_in, v_in, k_src, q_src, v_src,
           k_own, q_own, v_own, k_halo, v_halo, kn, vt, l_scr, s_scr, p_scr, start_scr, count_scr, o_src, o_own,
           load_s, k_rs, q_rs, v_rs, o_rs, send_s, halo_ss, halo_rs):
    planes, fold, grp, heads = cfg
    n = fold * grp
    cols = heads * HDIM
    pairs = n // 2
    wide_at, grp_at = lax.axis_index("wide"), lax.axis_index("grp")
    plane = wide_at // fold
    fold_at = wide_at % fold
    me = fold_at * grp + grp_at
    mine = me // 2
    mate = mine * 2 + 1 - me % 2
    has_prev, has_next = plane > 0, plane < planes - 1

    loads = [pltpu.make_async_copy(src, dst, load_s.at[i])
             for i, (src, dst) in enumerate(((k_hbm, k_in), (q_hbm, q_in), (v_hbm, v_in), (img_hbm, img)))]
    for load in loads:
        load.start()
    def device(at_plane, member):
        return (at_plane * fold + member // grp, member % grp)

    barrier = pltpu.get_barrier_semaphore()
    for i in range(1, n):
        pl.semaphore_signal(barrier, inc=1, device_id=device(plane, (me + i) % n), device_id_type=MESH)

    @pl.when(has_prev)
    def _():
        pl.semaphore_signal(barrier, inc=1, device_id=device(plane - 1, me), device_id_type=MESH)

    @pl.when(has_next)
    def _():
        pl.semaphore_signal(barrier, inc=1, device_id=device(plane + 1, me), device_id_type=MESH)
    def turn(ref, dst):
        whole = jnp.concatenate([ref[:, c:c + BLK].T for c in range(0, n * cols, BLK)], axis=0)
        for member in range(n):
            dst[member] = whole[member * cols:(member + 1) * cols]

    def remote(src, dst, ss, rs, dev):
        return pltpu.make_async_remote_copy(src_ref=src, dst_ref=dst, send_sem=ss, recv_sem=rs,
                                            device_id=dev, device_id_type=MESH)

    def exchange(src, dst, ss, rs):
        def send(to):
            remote(src.at[to], dst.at[me], ss, rs.at[mine % rs.shape[0]], device(plane, to)).start()

        def take(pair):
            remote(src.at[pl.ds(0, 2)], dst.at[pl.ds(2 * pair, 2)], ss, rs.at[pair], device(plane, mate)).wait_recv()

        def take_mate():
            remote(src.at[0], dst.at[mate], ss, rs.at[mine], device(plane, mate)).wait_recv()

        def take_all():
            part = src.at[pl.ds(0, n - 1)]
            remote(part, part, ss, rs.at[0], device(plane, mate)).wait_recv()

        def sent():
            part = src.at[pl.ds(0, n - 1)]
            remote(part, part, ss, rs.at[0], device(plane, mate)).wait_send()
        return send, take, take_mate, take_all, sent

    k_send, k_take, k_mate, _, _ = exchange(k_src, k_own, send_s.at[0], k_rs)
    q_send, q_take, q_mate, _, _ = exchange(q_src, q_own, send_s.at[0], q_rs)
    v_send, v_take, v_mate, _, _ = exchange(v_src, v_own, send_s.at[0], v_rs)

    def forward(which, halo, member, src, down_first=False):
        pair = member // 2

        def up():
            @pl.when(jnp.logical_and(has_next, member >= 1))
            def _():
                remote(src, halo.at[member - 1], halo_ss.at[which, 0], halo_rs.at[which, 0, pair],
                       device(plane + 1, me)).start()

        def down():
            @pl.when(jnp.logical_and(has_prev, member <= n - 2))
            def _():
                remote(src, halo.at[n - 1 + member], halo_ss.at[which, 1], halo_rs.at[which, 1, pair],
                       device(plane - 1, me)).start()

        for way in (down, up) if down_first else (up, down):
            way()

    def forward_pair(which, halo, pair, src):
        def up(first, count):
            remote(src.at[pl.ds(first, count)], halo.at[pl.ds(first - 1, count)], halo_ss.at[which, 0],
                   halo_rs.at[which, 0, pair], device(plane + 1, me)).start()

        def down(first, count):
            remote(src.at[pl.ds(first, count)], halo.at[pl.ds(n - 1 + first, count)], halo_ss.at[which, 1],
                   halo_rs.at[which, 1, pair], device(plane - 1, me)).start()

        @pl.when(jnp.logical_and(has_next, pair > 0))
        def _():
            up(2 * pair, 2)

        @pl.when(jnp.logical_and(has_next, pair == 0))
        def _():
            up(1, 1)

        @pl.when(jnp.logical_and(has_prev, pair < pairs - 1))
        def _():
            down(2 * pair, 2)

        @pl.when(jnp.logical_and(has_prev, pair == pairs - 1))
        def _():
            down(n - 2, 1)

    def landed(which, halo, way, pair, first, count):
        part = halo.at[pl.ds(first, count)]
        remote(part, part, halo_ss.at[which, way], halo_rs.at[which, way, pair], device(plane, mate)).wait_recv()

    def take_below(which, halo, pair, use):
        @pl.when(jnp.logical_and(has_prev, pair == 0))
        def _():
            landed(which, halo, 0, pair, 0, 1)
            use(0, halo.at[0])

        @pl.when(jnp.logical_and(has_prev, pair > 0))
        def _():
            landed(which, halo, 0, pair, 2 * pair - 1, 2)
            for r in range(2):
                use(2 * pair - 1 + r, halo.at[2 * pair - 1 + r])

    def take_above(which, halo, pair, use):
        @pl.when(jnp.logical_and(has_next, pair == pairs - 1))
        def _():
            landed(which, halo, 1, pair, 2 * n - 3, 1)
            use(3 * n - 3, halo.at[2 * n - 3])

        @pl.when(jnp.logical_and(has_next, pair < pairs - 1))
        def _():
            landed(which, halo, 1, pair, n - 1 + 2 * pair, 2)
            for r in range(2):
                use(2 * n - 1 + 2 * pair + r, halo.at[n - 1 + 2 * pair + r])

    def sent_up(which, halo):
        part = halo.at[pl.ds(0, n - 1)]
        remote(part, part, halo_ss.at[which, 0], halo_rs.at[which, 0], device(plane, mate)).wait_send()

    def sent_down(which, halo):
        part = halo.at[pl.ds(n - 1, n - 1)]
        remote(part, part, halo_ss.at[which, 1], halo_rs.at[which, 1], device(plane, mate)).wait_send()

    across = grp // 2
    fold_pair, grp_pair = mine // across, mine % across

    def to_pair(step):
        return (fold_pair + step // across) % fold * across + (grp_pair + step % across) % across

    def from_pair(step):
        return (fold_pair + fold - step // across) % fold * across + (grp_pair + across - step % across) % across

    def arrival(turn):
        return turn * across % (pairs - 1) + turn // (pairs - 1) * (pairs - 1)

    first_step = (fold - fold_pair) % fold * across + (across - grp_pair) % across

    def turn_order(turn):
        step = arrival(turn)
        other = jnp.where(step == 1, pairs - 1, jnp.where(step == pairs - 1, 1, step))
        return jnp.where(first_step == pairs - 1, other, step)

    def out_order(send):
        for turn in range(1, pairs):
            for r in (1, 0):
                send(2 * to_pair(arrival(turn)) + r)

    loads[0].wait()
    turn(k_in, k_src)
    pl.semaphore_wait(barrier, n - 1 + has_prev.astype(jnp.int32) + has_next.astype(jnp.int32))
    forward(0, k_halo, me, k_src.at[me])
    k_send(mate)
    out_order(k_send)
    loads[2].wait()
    turn(v_in, v_src)
    forward(1, v_halo, me, v_src.at[me], True)
    v_send(mate)
    loads[1].wait()
    turn(q_in, q_src)
    q_send(mate)
    out_order(v_send)
    def natural(slot, src):
        kn[slot] = src[...].T

    loads[3].wait()
    factor = math.log2(math.e) / math.sqrt(HDIM)
    blocks = img.shape[0]
    base = plane * n

    def span(block):
        own_id = img[block]
        before, after = jnp.int32(0), jnp.int32(0)
        for d in range(1, MOST):
            low = jnp.where(block >= d, img[jnp.maximum(block - d, 0)], -1)
            high = jnp.where(block + d < blocks, img[jnp.minimum(block + d, blocks - 1)], -1)
            before += (low == own_id).astype(jnp.int32)
            after += (high == own_id).astype(jnp.int32)
        return before, before + after + 1

    def note_span(m, carry):
        before, count = span(base + m)
        start_scr[m] = m + n - 1 - before
        count_scr[m] = count
        return carry

    lax.fori_loop(0, n, note_span, 0)
    natural(n - 1 + me, k_src.at[me])
    vt[n - 1 + me] = v_src[me]
    k_mate()
    forward(0, k_halo, mate, k_own.at[mate])
    v_mate()
    forward(1, v_halo, mate, v_own.at[mate], True)
    natural(n - 1 + mate, k_own.at[mate])
    vt[n - 1 + mate] = v_own[mate]
    def take_k(step, carry):
        pair = from_pair(arrival(step))
        k_take(pair)
        forward_pair(0, k_halo, pair, k_own)
        for r in range(2):
            natural(n - 1 + 2 * pair + r, k_own.at[2 * pair + r])
        return carry

    lax.fori_loop(1, pairs, take_k, 0)
    out_order(q_send)
    def take_v(step, carry):
        pair = from_pair(turn_order(step))
        v_take(pair)
        forward_pair(1, v_halo, pair, v_own)
        for r in range(2):
            vt[n - 1 + 2 * pair + r] = v_own[2 * pair + r]
        return carry

    lax.fori_loop(1, pairs, take_v, 0)
    def k_far(step, carry):
        take_below(0, k_halo, from_pair(arrival(step)), natural)
        take_above(0, k_halo, from_pair(arrival(step)), natural)
        return carry

    lax.fori_loop(0, pairs, k_far, 0)
    def scores(m, s_ref):
        start, count = start_scr[m], count_scr[m]
        rows = []
        for h in range(heads):
            q_h = q_own[m, h * HDIM:(h + 1) * HDIM]
            none = jnp.zeros_like(q_h)
            rows.append(jnp.concatenate([q_h if j == h else none for j in range(heads)], axis=1))
        q_all = jnp.concatenate(rows, axis=0)
        top = jnp.full((8, heads * BLK), NEG, jnp.float32)
        for t in range(MOST):
            s = jnp.dot(kn[start + jnp.where(t < count, t, 0)], q_all, preferred_element_type=jnp.float32)
            s_ref[t] = s
            high = jnp.max(s.reshape(BLK // 8, 8, heads * BLK), axis=0)
            top = jnp.maximum(top, jnp.where(t < count, high, NEG))
        return jnp.max(top, axis=0, keepdims=True), count

    def weigh(m, s_ref, top, count):
        total = jnp.zeros((8, heads * BLK), jnp.float32)
        for t in range(MOST):
            shift = jnp.where(t < count, -top * factor, NEG)
            w = jnp.exp2(s_ref[t] * factor + shift)
            total = total + jnp.sum(w.reshape(BLK // 8, 8, heads * BLK), axis=0)
            p_scr[m, t * BLK:(t + 1) * BLK] = w.astype(jnp.bfloat16)
        l_scr[m] = jnp.sum(total, axis=0, keepdims=True)

    def hold(slot, src):
        vt[slot] = src[...]

    o_send, _, _, o_take, o_sent = exchange(o_src, o_own, send_s.at[1], o_rs)

    def finish(pair, local=False, lead=0):
        for r in range(2):
            m = 2 * pair + r
            start, count = start_scr[m], count_scr[m]
            v = jnp.concatenate([vt[start + jnp.where(t < count, t, 0)] for t in range(MOST)], axis=1)
            res = jnp.dot(v, p_scr[m], preferred_element_type=jnp.float32)
            res = jnp.concatenate([res[h * HDIM:(h + 1) * HDIM, h * BLK:(h + 1) * BLK]
                                   / l_scr[m, :, h * BLK:(h + 1) * BLK] for h in range(heads)], axis=0)
            o_src[m] = res.astype(jnp.bfloat16)
        if not local:
            for r in range(2):
                o_send(2 * pair + (lead + r) % 2)

    q_own[me] = q_src[me]
    q_mate()
    pair = from_pair(0)
    now = scores(2 * pair, s_scr.at[0])
    for step in range(pairs):
        if step < pairs - 1:
            coming = from_pair(turn_order(step + 1))
            q_take(coming)
        later = scores(2 * pair + 1, s_scr.at[1])
        weigh(2 * pair, s_scr.at[0], *now)
        if step < pairs - 1:
            now = scores(2 * coming, s_scr.at[0])
        weigh(2 * pair + 1, s_scr.at[1], *later)
        pair = coming
        if step == pairs - 2:
            @pl.when(jnp.logical_not(has_prev))
            def _():
                take_above(1, v_halo, 0, hold)

                @pl.when(mine != 0)
                def _():
                    finish(0)
    @pl.when(has_prev)
    def _():
        for pair in range(pairs):
            take_below(1, v_halo, pair, hold)
        take_above(1, v_halo, 0, hold)

        @pl.when(mine != 0)
        def _():
            finish(0, lead=0)

    def leave(pair, carry):
        take_above(1, v_halo, pair, hold)

        @pl.when(pair != mine)
        def _():
            finish(pair, lead=me)
        return carry

    lax.fori_loop(1, pairs, leave, 0)
    finish(mine, True)
    o_send(mate)
    o_own[me] = o_src[me]
    part = vt.at[pl.ds(0, 3 * n - 3)]
    remote(part, part, send_s.at[0], k_rs.at[0], device(plane, mate)).wait_send()
    for which, halo in ((0, k_halo), (1, v_halo)):
        @pl.when(has_next)
        def _():
            sent_up(which, halo)

        @pl.when(has_prev)
        def _():
            sent_down(which, halo)
    o_take()
    flat = jnp.concatenate([o_own[member] for member in range(n)], axis=0)
    for c in range(0, n * cols, BLK):
        out[:, c:c + BLK] = flat[c:c + BLK].T
    o_sent()


def solution(mesh):
    wide, grp = mesh.shape["wide"], mesh.shape["grp"]
    fold = MOST // grp
    n = fold * grp
    planes = wide // fold

    def body(query_rows, key_rows, value_rows, block_image):
        rows, width = query_rows.shape
        heads = width // HDIM // n
        cols = heads * HDIM
        bf, f32 = jnp.bfloat16, jnp.float32
        hbm = pl.BlockSpec(memory_space=pltpu.HBM)
        dma = pltpu.SemaphoreType.DMA
        slices = pltpu.VMEM((n, cols, BLK), bf)
        halo = pltpu.VMEM((2 * n - 2, cols, BLK), bf)
        lanes = heads * BLK
        args = [pltpu.with_memory_space_constraint(a, pltpu.HBM)
                for a in (block_image, query_rows, key_rows, value_rows)]
        return pl.pallas_call(
            functools.partial(kernel, (planes, fold, grp, heads)),
            out_shape=jax.ShapeDtypeStruct((rows, width), bf),
            in_specs=[hbm] * 4,
            out_specs=pl.BlockSpec(memory_space=pltpu.VMEM),
            scratch_shapes=[pltpu.SMEM(block_image.shape, jnp.int32)]
            + [pltpu.VMEM((rows, width), bf)] * 3 + [slices] * 6 + [halo] * 2 + [
                pltpu.VMEM((3 * n - 2, BLK, cols), bf),
                pltpu.VMEM((3 * n - 2, cols, BLK), bf),
                pltpu.VMEM((n, 1, lanes), f32),
                pltpu.VMEM((4, MOST, BLK, lanes), f32),
                pltpu.VMEM((n, MOST * BLK, lanes), bf),
                pltpu.SMEM((n,), jnp.int32), pltpu.SMEM((n,), jnp.int32),
                slices, slices,
            ] + [dma((4,))] + [dma((n // 2,))] * 3 + [dma((1,)), dma((2,)), dma((2, 2)), dma((2, 2, n // 2))],
            compiler_params=pltpu.CompilerParams(collective_id=0, has_side_effects=True,
                                                 vmem_limit_bytes=40 << 20),
        )(*args)

    return jax.shard_map(
        body,
        mesh=mesh,
        in_specs=(
            P(("wide", "grp"), None),
            P(("wide", "grp"), None),
            P(("wide", "grp"), None),
            P(),
        ),
        out_specs=P(("wide", "grp"), None),
        check_vma=False,
    )
```

```python
import functools
import math

import jax
import jax.numpy as jnp
from jax import lax
from jax.experimental import pallas as pl
from jax.experimental.pallas import tpu as pltpu
from jax.sharding import PartitionSpec as P

HDIM = 80
BLK = 128
MOST = 8
NEG = -1e30
MESH = pl.DeviceIdType.MESH


def kernel(cfg, img_hbm, q_hbm, k_hbm, v_hbm, out, img, q_in, k_in, v_in, k_src, q_src, v_src,
           k_own, q_own, v_own, k_halo, v_halo, kn, vt, l_scr, s_scr, p_scr, start_scr, count_scr, o_src, o_own,
           load_s, k_rs, q_rs, v_rs, o_rs, send_s, halo_ss, halo_rs):
    planes, fold, grp, heads = cfg
    n = fold * grp
    cols = heads * HDIM
    pairs = n // 2
    wide_at, grp_at = lax.axis_index("wide"), lax.axis_index("grp")
    plane = wide_at // fold
    fold_at = wide_at % fold
    me = fold_at * grp + grp_at
    mine = me // 2
    mate = mine * 2 + 1 - me % 2
    has_prev, has_next = plane > 0, plane < planes - 1

    loads = [pltpu.make_async_copy(src, dst, load_s.at[i])
             for i, (src, dst) in enumerate(((k_hbm, k_in), (v_hbm, v_in), (q_hbm, q_in), (img_hbm, img)))]
    for load in loads:
        load.start()
    def device(at_plane, member):
        return (at_plane * fold + member // grp, member % grp)

    barrier = pltpu.get_barrier_semaphore()
    for i in range(1, n):
        pl.semaphore_signal(barrier, inc=1, device_id=device(plane, (me + i) % n), device_id_type=MESH)

    @pl.when(has_prev)
    def _():
        pl.semaphore_signal(barrier, inc=1, device_id=device(plane - 1, me), device_id_type=MESH)

    @pl.when(has_next)
    def _():
        pl.semaphore_signal(barrier, inc=1, device_id=device(plane + 1, me), device_id_type=MESH)
    def turn(ref, dst):
        whole = jnp.concatenate([ref[:, c:c + BLK].T for c in range(0, n * cols, BLK)], axis=0)
        for member in range(n):
            dst[member] = whole[member * cols:(member + 1) * cols]

    def remote(src, dst, ss, rs, dev):
        return pltpu.make_async_remote_copy(src_ref=src, dst_ref=dst, send_sem=ss, recv_sem=rs,
                                            device_id=dev, device_id_type=MESH)

    def exchange(src, dst, ss, rs):
        def send(to):
            remote(src.at[to], dst.at[me], ss, rs.at[mine % rs.shape[0]], device(plane, to)).start()

        def take(pair):
            remote(src.at[pl.ds(0, 2)], dst.at[pl.ds(2 * pair, 2)], ss, rs.at[pair], device(plane, mate)).wait_recv()

        def take_mate():
            remote(src.at[0], dst.at[mate], ss, rs.at[mine], device(plane, mate)).wait_recv()

        def take_all():
            part = src.at[pl.ds(0, n - 1)]
            remote(part, part, ss, rs.at[0], device(plane, mate)).wait_recv()

        def sent():
            part = src.at[pl.ds(0, n - 1)]
            remote(part, part, ss, rs.at[0], device(plane, mate)).wait_send()
        return send, take, take_mate, take_all, sent

    k_send, k_take, k_mate, _, _ = exchange(k_src, k_own, send_s.at[0], k_rs)
    q_send, q_take, q_mate, _, _ = exchange(q_src, q_own, send_s.at[0], q_rs)
    v_send, v_take, v_mate, _, _ = exchange(v_src, v_own, send_s.at[0], v_rs)

    def forward(which, halo, member, src, down_first=False):
        pair = member // 2

        def up():
            @pl.when(jnp.logical_and(has_next, member >= 1))
            def _():
                remote(src, halo.at[member - 1], halo_ss.at[which, 0], halo_rs.at[which, 0, pair],
                       device(plane + 1, me)).start()

        def down():
            @pl.when(jnp.logical_and(has_prev, member <= n - 2))
            def _():
                remote(src, halo.at[n - 1 + member], halo_ss.at[which, 1], halo_rs.at[which, 1, pair],
                       device(plane - 1, me)).start()

        for way in (down, up) if down_first else (up, down):
            way()

    def forward_pair(which, halo, pair, src):
        def up(first, count):
            remote(src.at[pl.ds(first, count)], halo.at[pl.ds(first - 1, count)], halo_ss.at[which, 0],
                   halo_rs.at[which, 0, pair], device(plane + 1, me)).start()

        def down(first, count):
            remote(src.at[pl.ds(first, count)], halo.at[pl.ds(n - 1 + first, count)], halo_ss.at[which, 1],
                   halo_rs.at[which, 1, pair], device(plane - 1, me)).start()

        @pl.when(jnp.logical_and(has_next, pair > 0))
        def _():
            up(2 * pair, 2)

        @pl.when(jnp.logical_and(has_next, pair == 0))
        def _():
            up(1, 1)

        @pl.when(jnp.logical_and(has_prev, pair < pairs - 1))
        def _():
            down(2 * pair, 2)

        @pl.when(jnp.logical_and(has_prev, pair == pairs - 1))
        def _():
            down(n - 2, 1)

    def landed(which, halo, way, pair, first, count):
        part = halo.at[pl.ds(first, count)]
        remote(part, part, halo_ss.at[which, way], halo_rs.at[which, way, pair], device(plane, mate)).wait_recv()

    def take_below(which, halo, pair, use):
        @pl.when(jnp.logical_and(has_prev, pair == 0))
        def _():
            landed(which, halo, 0, pair, 0, 1)
            use(0, halo.at[0])

        @pl.when(jnp.logical_and(has_prev, pair > 0))
        def _():
            landed(which, halo, 0, pair, 2 * pair - 1, 2)
            for r in range(2):
                use(2 * pair - 1 + r, halo.at[2 * pair - 1 + r])

    def take_above(which, halo, pair, use):
        @pl.when(jnp.logical_and(has_next, pair == pairs - 1))
        def _():
            landed(which, halo, 1, pair, 2 * n - 3, 1)
            use(3 * n - 3, halo.at[2 * n - 3])

        @pl.when(jnp.logical_and(has_next, pair < pairs - 1))
        def _():
            landed(which, halo, 1, pair, n - 1 + 2 * pair, 2)
            for r in range(2):
                use(2 * n - 1 + 2 * pair + r, halo.at[n - 1 + 2 * pair + r])

    def sent_up(which, halo):
        part = halo.at[pl.ds(0, n - 1)]
        remote(part, part, halo_ss.at[which, 0], halo_rs.at[which, 0], device(plane, mate)).wait_send()

    def sent_down(which, halo):
        part = halo.at[pl.ds(n - 1, n - 1)]
        remote(part, part, halo_ss.at[which, 1], halo_rs.at[which, 1], device(plane, mate)).wait_send()

    across = grp // 2
    fold_pair, grp_pair = mine // across, mine % across

    def to_pair(step):
        return (fold_pair + step // across) % fold * across + (grp_pair + step % across) % across

    def from_pair(step):
        return (fold_pair + fold - step // across) % fold * across + (grp_pair + across - step % across) % across

    def arrival(turn):
        return turn * across % (pairs - 1) + turn // (pairs - 1) * (pairs - 1)

    first_step = (fold - fold_pair) % fold * across + (across - grp_pair) % across

    def turn_order(turn):
        step = arrival(turn)
        other = jnp.where(step == 1, pairs - 1, jnp.where(step == pairs - 1, 1, step))
        return jnp.where(first_step == pairs - 1, other, step)

    def out_order(send):
        for turn in range(1, pairs):
            for r in (1, 0):
                send(2 * to_pair(arrival(turn)) + r)

    loads[0].wait()
    turn(k_in, k_src)
    pl.semaphore_wait(barrier, n - 1 + has_prev.astype(jnp.int32) + has_next.astype(jnp.int32))
    forward(0, k_halo, me, k_src.at[me])
    k_send(mate)
    out_order(k_send)
    loads[1].wait()
    turn(v_in, v_src)
    forward(1, v_halo, me, v_src.at[me], True)
    v_send(mate)
    loads[2].wait()
    turn(q_in, q_src)
    q_send(mate)
    out_order(v_send)
    def natural(slot, src):
        kn[slot] = src[...].T

    loads[3].wait()
    factor = math.log2(math.e) / math.sqrt(HDIM)
    blocks = img.shape[0]
    base = plane * n

    def span(block):
        own_id = img[block]
        before, after = jnp.int32(0), jnp.int32(0)
        for d in range(1, MOST):
            low = jnp.where(block >= d, img[jnp.maximum(block - d, 0)], -1)
            high = jnp.where(block + d < blocks, img[jnp.minimum(block + d, blocks - 1)], -1)
            before += (low == own_id).astype(jnp.int32)
            after += (high == own_id).astype(jnp.int32)
        return before, before + after + 1

    def note_span(m, carry):
        before, count = span(base + m)
        start_scr[m] = m + n - 1 - before
        count_scr[m] = count
        return carry

    lax.fori_loop(0, n, note_span, 0)
    natural(n - 1 + me, k_src.at[me])
    vt[n - 1 + me] = v_src[me]
    k_mate()
    forward(0, k_halo, mate, k_own.at[mate])
    v_mate()
    forward(1, v_halo, mate, v_own.at[mate], True)
    natural(n - 1 + mate, k_own.at[mate])
    vt[n - 1 + mate] = v_own[mate]
    def take_k(step, carry):
        pair = from_pair(arrival(step))
        k_take(pair)
        forward_pair(0, k_halo, pair, k_own)
        for r in range(2):
            natural(n - 1 + 2 * pair + r, k_own.at[2 * pair + r])
        return carry

    lax.fori_loop(1, pairs, take_k, 0)
    out_order(q_send)
    def take_v(step, carry):
        pair = from_pair(turn_order(step))
        v_take(pair)
        forward_pair(1, v_halo, pair, v_own)
        for r in range(2):
            vt[n - 1 + 2 * pair + r] = v_own[2 * pair + r]
        return carry

    lax.fori_loop(1, pairs, take_v, 0)
    def k_far(step, carry):
        take_below(0, k_halo, from_pair(arrival(step)), natural)
        take_above(0, k_halo, from_pair(arrival(step)), natural)
        return carry

    lax.fori_loop(0, pairs, k_far, 0)
    def scores(m, s_ref):
        start, count = start_scr[m], count_scr[m]
        rows = []
        for h in range(heads):
            q_h = q_own[m, h * HDIM:(h + 1) * HDIM]
            none = jnp.zeros_like(q_h)
            rows.append(jnp.concatenate([q_h if j == h else none for j in range(heads)], axis=1))
        q_all = jnp.concatenate(rows, axis=0)
        top = jnp.full((8, heads * BLK), NEG, jnp.float32)
        for t in range(MOST):
            s = jnp.dot(kn[start + jnp.where(t < count, t, 0)], q_all, preferred_element_type=jnp.float32)
            s_ref[t] = s
            high = jnp.max(s.reshape(BLK // 8, 8, heads * BLK), axis=0)
            top = jnp.maximum(top, jnp.where(t < count, high, NEG))
        return jnp.max(top, axis=0, keepdims=True), count

    def weigh(m, s_ref, top, count):
        total = jnp.zeros((8, heads * BLK), jnp.float32)
        for t in range(MOST):
            shift = jnp.where(t < count, -top * factor, NEG)
            w = jnp.exp2(s_ref[t] * factor + shift)
            total = total + jnp.sum(w.reshape(BLK // 8, 8, heads * BLK), axis=0)
            p_scr[m, t * BLK:(t + 1) * BLK] = w.astype(jnp.bfloat16)
        l_scr[m] = jnp.sum(total, axis=0, keepdims=True)

    def hold(slot, src):
        vt[slot] = src[...]

    _, _, _, _, o_sent = exchange(o_src, o_own, send_s.at[1], o_rs)

    def o_send(to):
        away = (to // grp + fold - fold_at) % fold
        remote(o_src.at[to], o_own.at[me], send_s.at[1], o_rs.at[(away + fold - 1) // fold],
               device(plane, to)).start()


    def finish(pair, local=False, lead=0):
        for r in range(2):
            m = 2 * pair + r
            start, count = start_scr[m], count_scr[m]
            v = jnp.concatenate([vt[start + jnp.where(t < count, t, 0)] for t in range(MOST)], axis=1)
            res = jnp.dot(v, p_scr[m], preferred_element_type=jnp.float32)
            res = jnp.concatenate([res[h * HDIM:(h + 1) * HDIM, h * BLK:(h + 1) * BLK]
                                   / l_scr[m, :, h * BLK:(h + 1) * BLK] for h in range(heads)], axis=0)
            o_src[m] = res.astype(jnp.bfloat16)
        if not local:
            for r in range(2):
                o_send(2 * pair + (lead + r) % 2)

    q_own[me] = q_src[me]
    q_mate()
    pair = from_pair(0)
    now = scores(2 * pair, s_scr.at[0])
    for step in range(pairs):
        if step < pairs - 1:
            coming = from_pair(turn_order(step + 1))
            q_take(coming)
        later = scores(2 * pair + 1, s_scr.at[1])
        weigh(2 * pair, s_scr.at[0], *now)
        if step < pairs - 1:
            now = scores(2 * coming, s_scr.at[0])
        weigh(2 * pair + 1, s_scr.at[1], *later)
        pair = coming
        if step == pairs - 2:
            @pl.when(jnp.logical_not(has_prev))
            def _():
                take_above(1, v_halo, 0, hold)

                @pl.when(mine != 0)
                def _():
                    finish(0)
    @pl.when(has_prev)
    def _():
        for pair in range(pairs):
            take_below(1, v_halo, pair, hold)
        take_above(1, v_halo, 0, hold)

        @pl.when(mine != 0)
        def _():
            finish(0, lead=0)

    def leave(pair, carry):
        take_above(1, v_halo, pair, hold)

        @pl.when(pair != mine)
        def _():
            finish(pair, lead=me)
        return carry

    lax.fori_loop(1, pairs, leave, 0)
    finish(mine, True)
    o_send(mate)
    o_own[me] = o_src[me]
    part = vt.at[pl.ds(0, 3 * n - 3)]
    remote(part, part, send_s.at[0], k_rs.at[0], device(plane, mate)).wait_send()
    for which, halo in ((0, k_halo), (1, v_halo)):
        @pl.when(has_next)
        def _():
            sent_up(which, halo)

        @pl.when(has_prev)
        def _():
            sent_down(which, halo)
    half = n // fold
    width = half * cols

    def settle(which, count):
        part = o_own.at[pl.ds(0, count)]
        remote(part, part, send_s.at[1], o_rs.at[which], device(plane, mate)).wait_recv()
        for f in range(1, fold) if which else range(1):
            at = (fold_at + f) % fold
            flat = jnp.concatenate([o_own[at * half + i] for i in range(half)], axis=0)
            for c in range(0, width, BLK):
                out[:, pl.ds(pl.multiple_of(at * width + c, BLK), BLK)] = flat[c:c + BLK].T

    settle(0, half - 1)
    settle(1, n - half)
    o_sent()


def solution(mesh):
    wide, grp = mesh.shape["wide"], mesh.shape["grp"]
    fold = MOST // grp
    n = fold * grp
    planes = wide // fold

    def body(query_rows, key_rows, value_rows, block_image):
        rows, width = query_rows.shape
        heads = width // HDIM // n
        cols = heads * HDIM
        bf, f32 = jnp.bfloat16, jnp.float32
        hbm = pl.BlockSpec(memory_space=pltpu.HBM)
        dma = pltpu.SemaphoreType.DMA
        slices = pltpu.VMEM((n, cols, BLK), bf)
        halo = pltpu.VMEM((2 * n - 2, cols, BLK), bf)
        lanes = heads * BLK
        args = [pltpu.with_memory_space_constraint(a, pltpu.HBM)
                for a in (block_image, query_rows, key_rows, value_rows)]
        return pl.pallas_call(
            functools.partial(kernel, (planes, fold, grp, heads)),
            out_shape=jax.ShapeDtypeStruct((rows, width), bf),
            in_specs=[hbm] * 4,
            out_specs=pl.BlockSpec(memory_space=pltpu.VMEM),
            scratch_shapes=[pltpu.SMEM(block_image.shape, jnp.int32)]
            + [pltpu.VMEM((rows, width), bf)] * 3 + [slices] * 6 + [halo] * 2 + [
                pltpu.VMEM((3 * n - 2, BLK, cols), bf),
                pltpu.VMEM((3 * n - 2, cols, BLK), bf),
                pltpu.VMEM((n, 1, lanes), f32),
                pltpu.VMEM((4, MOST, BLK, lanes), f32),
                pltpu.VMEM((n, MOST * BLK, lanes), bf),
                pltpu.SMEM((n,), jnp.int32), pltpu.SMEM((n,), jnp.int32),
                slices, slices,
            ] + [dma((4,))] + [dma((n // 2,))] * 3 + [dma((2,)), dma((2,)), dma((2, 2)), dma((2, 2, n // 2))],
            compiler_params=pltpu.CompilerParams(collective_id=0, has_side_effects=True,
                                                 vmem_limit_bytes=40 << 20),
        )(*args)

    return jax.shard_map(
        body,
        mesh=mesh,
        in_specs=(
            P(("wide", "grp"), None),
            P(("wide", "grp"), None),
            P(("wide", "grp"), None),
            P(),
        ),
        out_specs=P(("wide", "grp"), None),
        check_vma=False,
    )
```

```python
import functools
import math

import jax
import jax.numpy as jnp
from jax import lax
from jax.experimental import pallas as pl
from jax.experimental.pallas import tpu as pltpu
from jax.sharding import PartitionSpec as P

HDIM = 80
BLK = 128
MOST = 8
NEG = -1e30
MESH = pl.DeviceIdType.MESH


def kernel(cfg, img_hbm, q_hbm, k_hbm, v_hbm, out, img, q_in, k_in, v_in, k_src, q_src, v_src,
           k_own, q_own, v_own, k_halo, v_halo, kn, vt, l_scr, s_scr, p_scr, start_scr, count_scr, o_src, o_own,
           load_s, k_rs, q_rs, v_rs, o_rs, send_s, halo_ss, halo_rs):
    planes, fold, grp, heads = cfg
    n = fold * grp
    cols = heads * HDIM
    pairs = n // 2
    wide_at, grp_at = lax.axis_index("wide"), lax.axis_index("grp")
    plane = wide_at // fold
    fold_at = wide_at % fold
    me = fold_at * grp + grp_at
    mine = me // 2
    mate = mine * 2 + 1 - me % 2
    has_prev, has_next = plane > 0, plane < planes - 1

    loads = [pltpu.make_async_copy(src, dst, load_s.at[i])
             for i, (src, dst) in enumerate(((k_hbm, k_in), (v_hbm, v_in), (q_hbm, q_in), (img_hbm, img)))]
    for load in loads:
        load.start()
    def device(at_plane, member):
        return (at_plane * fold + member // grp, member % grp)

    barrier = pltpu.get_barrier_semaphore()
    for i in range(1, n):
        pl.semaphore_signal(barrier, inc=1, device_id=device(plane, (me + i) % n), device_id_type=MESH)

    @pl.when(has_prev)
    def _():
        pl.semaphore_signal(barrier, inc=1, device_id=device(plane - 1, me), device_id_type=MESH)

    @pl.when(has_next)
    def _():
        pl.semaphore_signal(barrier, inc=1, device_id=device(plane + 1, me), device_id_type=MESH)
    def turn(ref, dst):
        whole = jnp.concatenate([ref[:, c:c + BLK].T for c in range(0, n * cols, BLK)], axis=0)
        for member in range(n):
            dst[member] = whole[member * cols:(member + 1) * cols]

    def remote(src, dst, ss, rs, dev):
        return pltpu.make_async_remote_copy(src_ref=src, dst_ref=dst, send_sem=ss, recv_sem=rs,
                                            device_id=dev, device_id_type=MESH)

    def exchange(src, dst, ss, rs):
        def send(to):
            remote(src.at[to], dst.at[me], ss, rs.at[mine % rs.shape[0]], device(plane, to)).start()

        def take(pair):
            remote(src.at[pl.ds(0, 2)], dst.at[pl.ds(2 * pair, 2)], ss, rs.at[pair], device(plane, mate)).wait_recv()

        def take_mate():
            remote(src.at[0], dst.at[mate], ss, rs.at[mine], device(plane, mate)).wait_recv()

        def take_all():
            part = src.at[pl.ds(0, n - 1)]
            remote(part, part, ss, rs.at[0], device(plane, mate)).wait_recv()

        def sent():
            part = src.at[pl.ds(0, n - 1)]
            remote(part, part, ss, rs.at[0], device(plane, mate)).wait_send()
        return send, take, take_mate, take_all, sent

    k_send, k_take, k_mate, _, _ = exchange(k_src, k_own, send_s.at[0], k_rs)
    q_send, q_take, q_mate, _, _ = exchange(q_src, q_own, send_s.at[0], q_rs)
    v_send, v_take, v_mate, _, _ = exchange(v_src, v_own, send_s.at[0], v_rs)

    def forward(which, halo, member, src, down_first=False):
        pair = member // 2

        def up():
            @pl.when(jnp.logical_and(has_next, member >= 1))
            def _():
                remote(src, halo.at[member - 1], halo_ss.at[which, 0], halo_rs.at[which, 0, pair],
                       device(plane + 1, me)).start()

        def down():
            @pl.when(jnp.logical_and(has_prev, member <= n - 2))
            def _():
                remote(src, halo.at[n - 1 + member], halo_ss.at[which, 1], halo_rs.at[which, 1, pair],
                       device(plane - 1, me)).start()

        for way in (down, up) if down_first else (up, down):
            way()

    def forward_pair(which, halo, pair, src):
        def up(first, count):
            remote(src.at[pl.ds(first, count)], halo.at[pl.ds(first - 1, count)], halo_ss.at[which, 0],
                   halo_rs.at[which, 0, pair], device(plane + 1, me)).start()

        def down(first, count):
            remote(src.at[pl.ds(first, count)], halo.at[pl.ds(n - 1 + first, count)], halo_ss.at[which, 1],
                   halo_rs.at[which, 1, pair], device(plane - 1, me)).start()

        @pl.when(jnp.logical_and(has_next, pair > 0))
        def _():
            up(2 * pair, 2)

        @pl.when(jnp.logical_and(has_next, pair == 0))
        def _():
            up(1, 1)

        @pl.when(jnp.logical_and(has_prev, pair < pairs - 1))
        def _():
            down(2 * pair, 2)

        @pl.when(jnp.logical_and(has_prev, pair == pairs - 1))
        def _():
            down(n - 2, 1)

    def landed(which, halo, way, pair, first, count):
        part = halo.at[pl.ds(first, count)]
        remote(part, part, halo_ss.at[which, way], halo_rs.at[which, way, pair], device(plane, mate)).wait_recv()

    def take_below(which, halo, pair, use):
        @pl.when(jnp.logical_and(has_prev, pair == 0))
        def _():
            landed(which, halo, 0, pair, 0, 1)
            use(0, halo.at[0])

        @pl.when(jnp.logical_and(has_prev, pair > 0))
        def _():
            landed(which, halo, 0, pair, 2 * pair - 1, 2)
            for r in range(2):
                use(2 * pair - 1 + r, halo.at[2 * pair - 1 + r])

    def take_above(which, halo, pair, use):
        @pl.when(jnp.logical_and(has_next, pair == pairs - 1))
        def _():
            landed(which, halo, 1, pair, 2 * n - 3, 1)
            use(3 * n - 3, halo.at[2 * n - 3])

        @pl.when(jnp.logical_and(has_next, pair < pairs - 1))
        def _():
            landed(which, halo, 1, pair, n - 1 + 2 * pair, 2)
            for r in range(2):
                use(2 * n - 1 + 2 * pair + r, halo.at[n - 1 + 2 * pair + r])

    def sent_up(which, halo):
        part = halo.at[pl.ds(0, n - 1)]
        remote(part, part, halo_ss.at[which, 0], halo_rs.at[which, 0], device(plane, mate)).wait_send()

    def sent_down(which, halo):
        part = halo.at[pl.ds(n - 1, n - 1)]
        remote(part, part, halo_ss.at[which, 1], halo_rs.at[which, 1], device(plane, mate)).wait_send()

    across = grp // 2
    fold_pair, grp_pair = mine // across, mine % across

    def to_pair(step):
        return (fold_pair + step // across) % fold * across + (grp_pair + step % across) % across

    def from_pair(step):
        return (fold_pair + fold - step // across) % fold * across + (grp_pair + across - step % across) % across

    def arrival(turn):
        return turn * across % (pairs - 1) + turn // (pairs - 1) * (pairs - 1)

    first_step = (fold - fold_pair) % fold * across + (across - grp_pair) % across

    def turn_order(turn):
        step = arrival(turn)
        other = jnp.where(step == 1, pairs - 1, jnp.where(step == pairs - 1, 1, step))
        return jnp.where(first_step == pairs - 1, other, step)

    def out_order(send, cores=(1, 0)):
        for turn in range(1, pairs):
            for r in cores:
                send(2 * to_pair(arrival(turn)) + r)

    loads[0].wait()
    turn(k_in, k_src)
    pl.semaphore_wait(barrier, n - 1 + has_prev.astype(jnp.int32) + has_next.astype(jnp.int32))
    forward(0, k_halo, me, k_src.at[me])
    k_send(mate)
    out_order(k_send)
    loads[1].wait()
    turn(v_in, v_src)
    forward(1, v_halo, me, v_src.at[me], True)
    v_send(mate)
    loads[2].wait()
    turn(q_in, q_src)
    q_send(mate)
    out_order(v_send)
    def natural(slot, src):
        kn[slot] = src[...].T

    loads[3].wait()
    factor = math.log2(math.e) / math.sqrt(HDIM)
    blocks = img.shape[0]
    base = plane * n

    def span(block):
        own_id = img[block]
        before, after = jnp.int32(0), jnp.int32(0)
        for d in range(1, MOST):
            low = jnp.where(block >= d, img[jnp.maximum(block - d, 0)], -1)
            high = jnp.where(block + d < blocks, img[jnp.minimum(block + d, blocks - 1)], -1)
            before += (low == own_id).astype(jnp.int32)
            after += (high == own_id).astype(jnp.int32)
        return before, before + after + 1

    def note_span(m, carry):
        before, count = span(base + m)
        start_scr[m] = m + n - 1 - before
        count_scr[m] = count
        return carry

    lax.fori_loop(0, n, note_span, 0)
    natural(n - 1 + me, k_src.at[me])
    vt[n - 1 + me] = v_src[me]
    k_mate()
    forward(0, k_halo, mate, k_own.at[mate])
    v_mate()
    forward(1, v_halo, mate, v_own.at[mate], True)
    natural(n - 1 + mate, k_own.at[mate])
    vt[n - 1 + mate] = v_own[mate]
    def take_k(step, carry):
        pair = from_pair(arrival(step))
        k_take(pair)
        forward_pair(0, k_halo, pair, k_own)
        for r in range(2):
            natural(n - 1 + 2 * pair + r, k_own.at[2 * pair + r])
        return carry

    lax.fori_loop(1, pairs, take_k, 0)
    out_order(q_send, (1,))
    out_order(q_send, (0,))
    def take_v(step, carry):
        pair = from_pair(turn_order(step))
        v_take(pair)
        forward_pair(1, v_halo, pair, v_own)
        for r in range(2):
            vt[n - 1 + 2 * pair + r] = v_own[2 * pair + r]
        return carry

    lax.fori_loop(1, pairs, take_v, 0)
    def k_far(step, carry):
        take_below(0, k_halo, from_pair(arrival(step)), natural)
        take_above(0, k_halo, from_pair(arrival(step)), natural)
        return carry

    lax.fori_loop(0, pairs, k_far, 0)
    def scores(m, s_ref):
        start, count = start_scr[m], count_scr[m]
        rows = []
        for h in range(heads):
            q_h = q_own[m, h * HDIM:(h + 1) * HDIM]
            none = jnp.zeros_like(q_h)
            rows.append(jnp.concatenate([q_h if j == h else none for j in range(heads)], axis=1))
        q_all = jnp.concatenate(rows, axis=0)
        top = jnp.full((8, heads * BLK), NEG, jnp.float32)
        for t in range(MOST):
            s = jnp.dot(kn[start + jnp.where(t < count, t, 0)], q_all, preferred_element_type=jnp.float32)
            s_ref[t] = s
            high = jnp.max(s.reshape(BLK // 8, 8, heads * BLK), axis=0)
            top = jnp.maximum(top, jnp.where(t < count, high, NEG))
        return jnp.max(top, axis=0, keepdims=True), count

    def weigh(m, s_ref, top, count):
        total = jnp.zeros((8, heads * BLK), jnp.float32)
        for t in range(MOST):
            shift = jnp.where(t < count, -top * factor, NEG)
            w = jnp.exp2(s_ref[t] * factor + shift)
            total = total + jnp.sum(w.reshape(BLK // 8, 8, heads * BLK), axis=0)
            p_scr[m, t * BLK:(t + 1) * BLK] = w.astype(jnp.bfloat16)
        l_scr[m] = jnp.sum(total, axis=0, keepdims=True)

    def hold(slot, src):
        vt[slot] = src[...]

    _, _, _, _, o_sent = exchange(o_src, o_own, send_s.at[1], o_rs)

    def o_send(to):
        away = (to // grp + fold - fold_at) % fold
        remote(o_src.at[to], o_own.at[me], send_s.at[1], o_rs.at[(away + fold - 1) // fold],
               device(plane, to)).start()


    def finish(pair, local=False, lead=0):
        for r in range(2):
            m = 2 * pair + r
            start, count = start_scr[m], count_scr[m]
            v = jnp.concatenate([vt[start + jnp.where(t < count, t, 0)] for t in range(MOST)], axis=1)
            res = jnp.dot(v, p_scr[m], preferred_element_type=jnp.float32)
            res = jnp.concatenate([res[h * HDIM:(h + 1) * HDIM, h * BLK:(h + 1) * BLK]
                                   / l_scr[m, :, h * BLK:(h + 1) * BLK] for h in range(heads)], axis=0)
            o_src[m] = res.astype(jnp.bfloat16)
        if not local:
            for r in range(2):
                o_send(2 * pair + (lead + r) % 2)

    q_own[me] = q_src[me]
    q_mate()
    pair = from_pair(0)
    now = scores(2 * pair, s_scr.at[0])
    for step in range(pairs):
        if step < pairs - 1:
            coming = from_pair(turn_order(step + 1))
            q_take(coming)
        later = scores(2 * pair + 1, s_scr.at[1])
        weigh(2 * pair, s_scr.at[0], *now)
        if step < pairs - 1:
            now = scores(2 * coming, s_scr.at[0])
        weigh(2 * pair + 1, s_scr.at[1], *later)
        pair = coming
        if step == pairs - 2:
            @pl.when(jnp.logical_not(has_prev))
            def _():
                take_above(1, v_halo, 0, hold)

                @pl.when(mine != 0)
                def _():
                    finish(0)
    @pl.when(has_prev)
    def _():
        for pair in range(pairs):
            take_below(1, v_halo, pair, hold)
        take_above(1, v_halo, 0, hold)

        @pl.when(mine != 0)
        def _():
            finish(0, lead=0)

    def leave(pair, carry):
        take_above(1, v_halo, pair, hold)

        @pl.when(pair != mine)
        def _():
            finish(pair, lead=me)
        return carry

    lax.fori_loop(1, pairs, leave, 0)
    finish(mine, True)
    o_send(mate)
    o_own[me] = o_src[me]
    part = vt.at[pl.ds(0, 3 * n - 3)]
    remote(part, part, send_s.at[0], k_rs.at[0], device(plane, mate)).wait_send()
    for which, halo in ((0, k_halo), (1, v_halo)):
        @pl.when(has_next)
        def _():
            sent_up(which, halo)

        @pl.when(has_prev)
        def _():
            sent_down(which, halo)
    half = n // fold
    width = half * cols

    def settle(which, count):
        part = o_own.at[pl.ds(0, count)]
        remote(part, part, send_s.at[1], o_rs.at[which], device(plane, mate)).wait_recv()
        for f in range(1, fold) if which else range(1):
            at = (fold_at + f) % fold
            flat = jnp.concatenate([o_own[at * half + i] for i in range(half)], axis=0)
            for c in range(0, width, BLK):
                out[:, pl.ds(pl.multiple_of(at * width + c, BLK), BLK)] = flat[c:c + BLK].T

    settle(0, half - 1)
    settle(1, n - half)
    o_sent()


def solution(mesh):
    wide, grp = mesh.shape["wide"], mesh.shape["grp"]
    fold = MOST // grp
    n = fold * grp
    planes = wide // fold

    def body(query_rows, key_rows, value_rows, block_image):
        rows, width = query_rows.shape
        heads = width // HDIM // n
        cols = heads * HDIM
        bf, f32 = jnp.bfloat16, jnp.float32
        hbm = pl.BlockSpec(memory_space=pltpu.HBM)
        dma = pltpu.SemaphoreType.DMA
        slices = pltpu.VMEM((n, cols, BLK), bf)
        halo = pltpu.VMEM((2 * n - 2, cols, BLK), bf)
        lanes = heads * BLK
        args = [pltpu.with_memory_space_constraint(a, pltpu.HBM)
                for a in (block_image, query_rows, key_rows, value_rows)]
        return pl.pallas_call(
            functools.partial(kernel, (planes, fold, grp, heads)),
            out_shape=jax.ShapeDtypeStruct((rows, width), bf),
            in_specs=[hbm] * 4,
            out_specs=pl.BlockSpec(memory_space=pltpu.VMEM),
            scratch_shapes=[pltpu.SMEM(block_image.shape, jnp.int32)]
            + [pltpu.VMEM((rows, width), bf)] * 3 + [slices] * 6 + [halo] * 2 + [
                pltpu.VMEM((3 * n - 2, BLK, cols), bf),
                pltpu.VMEM((3 * n - 2, cols, BLK), bf),
                pltpu.VMEM((n, 1, lanes), f32),
                pltpu.VMEM((4, MOST, BLK, lanes), f32),
                pltpu.VMEM((n, MOST * BLK, lanes), bf),
                pltpu.SMEM((n,), jnp.int32), pltpu.SMEM((n,), jnp.int32),
                slices, slices,
            ] + [dma((4,))] + [dma((n // 2,))] * 3 + [dma((2,)), dma((2,)), dma((2, 2)), dma((2, 2, n // 2))],
            compiler_params=pltpu.CompilerParams(collective_id=0, has_side_effects=True,
                                                 vmem_limit_bytes=40 << 20),
        )(*args)

    return jax.shard_map(
        body,
        mesh=mesh,
        in_specs=(
            P(("wide", "grp"), None),
            P(("wide", "grp"), None),
            P(("wide", "grp"), None),
            P(),
        ),
        out_specs=P(("wide", "grp"), None),
        check_vma=False,
    )
```

```python
import functools
import math

import jax
import jax.numpy as jnp
from jax import lax
from jax.experimental import pallas as pl
from jax.experimental.pallas import tpu as pltpu
from jax.sharding import PartitionSpec as P

HDIM = 80
BLK = 128
MOST = 8
NEG = -1e30
MESH = pl.DeviceIdType.MESH


def kernel(cfg, img_hbm, q_hbm, k_hbm, v_hbm, out, img, q_in, k_in, v_in, k_src, q_src, v_src,
           k_own, q_own, v_own, k_halo, v_halo, kn, vt, l_scr, s_scr, p_scr, start_scr, count_scr, o_src, o_own,
           load_s, k_rs, q_rs, v_rs, o_rs, send_s, halo_ss, halo_rs):
    planes, fold, grp, heads = cfg
    n = fold * grp
    cols = heads * HDIM
    pairs = n // 2
    wide_at, grp_at = lax.axis_index("wide"), lax.axis_index("grp")
    plane = wide_at // fold
    fold_at = wide_at % fold
    me = fold_at * grp + grp_at
    mine = me // 2
    mate = mine * 2 + 1 - me % 2
    has_prev, has_next = plane > 0, plane < planes - 1

    loads = [pltpu.make_async_copy(src, dst, load_s.at[i])
             for i, (src, dst) in enumerate(((k_hbm, k_in), (v_hbm, v_in), (q_hbm, q_in), (img_hbm, img)))]
    for load in loads:
        load.start()
    def device(at_plane, member):
        return (at_plane * fold + member // grp, member % grp)

    barrier = pltpu.get_barrier_semaphore()
    for i in range(1, n):
        pl.semaphore_signal(barrier, inc=1, device_id=device(plane, (me + i) % n), device_id_type=MESH)

    @pl.when(has_prev)
    def _():
        pl.semaphore_signal(barrier, inc=1, device_id=device(plane - 1, me), device_id_type=MESH)

    @pl.when(has_next)
    def _():
        pl.semaphore_signal(barrier, inc=1, device_id=device(plane + 1, me), device_id_type=MESH)
    def turn(ref, dst):
        whole = jnp.concatenate([ref[:, c:c + BLK].T for c in range(0, n * cols, BLK)], axis=0)
        for member in range(n):
            dst[member] = whole[member * cols:(member + 1) * cols]

    def remote(src, dst, ss, rs, dev):
        return pltpu.make_async_remote_copy(src_ref=src, dst_ref=dst, send_sem=ss, recv_sem=rs,
                                            device_id=dev, device_id_type=MESH)

    def exchange(src, dst, ss, rs):
        def send(to):
            remote(src.at[to], dst.at[me], ss, rs.at[mine % rs.shape[0]], device(plane, to)).start()

        def take(pair):
            remote(src.at[pl.ds(0, 2)], dst.at[pl.ds(2 * pair, 2)], ss, rs.at[pair], device(plane, mate)).wait_recv()

        def take_mate():
            remote(src.at[0], dst.at[mate], ss, rs.at[mine], device(plane, mate)).wait_recv()

        def take_all():
            part = src.at[pl.ds(0, n - 1)]
            remote(part, part, ss, rs.at[0], device(plane, mate)).wait_recv()

        def sent():
            part = src.at[pl.ds(0, n - 1)]
            remote(part, part, ss, rs.at[0], device(plane, mate)).wait_send()
        return send, take, take_mate, take_all, sent

    k_send, k_take, k_mate, _, _ = exchange(k_src, k_own, send_s.at[0], k_rs)
    q_send, q_take, q_mate, _, _ = exchange(q_src, q_own, send_s.at[0], q_rs)
    v_send, v_take, v_mate, _, _ = exchange(v_src, v_own, send_s.at[0], v_rs)

    def forward(which, halo, member, src, down_first=False):
        pair = member // 2

        def up():
            @pl.when(jnp.logical_and(has_next, member >= 1))
            def _():
                remote(src, halo.at[member - 1], halo_ss.at[which, 0], halo_rs.at[which, 0, pair],
                       device(plane + 1, me)).start()

        def down():
            @pl.when(jnp.logical_and(has_prev, member <= n - 2))
            def _():
                remote(src, halo.at[n - 1 + member], halo_ss.at[which, 1], halo_rs.at[which, 1, pair],
                       device(plane - 1, me)).start()

        for way in (down, up) if down_first else (up, down):
            way()

    def forward_pair(which, halo, pair, src):
        def up(first, count):
            remote(src.at[pl.ds(first, count)], halo.at[pl.ds(first - 1, count)], halo_ss.at[which, 0],
                   halo_rs.at[which, 0, pair], device(plane + 1, me)).start()

        def down(first, count):
            remote(src.at[pl.ds(first, count)], halo.at[pl.ds(n - 1 + first, count)], halo_ss.at[which, 1],
                   halo_rs.at[which, 1, pair], device(plane - 1, me)).start()

        @pl.when(jnp.logical_and(has_next, pair > 0))
        def _():
            up(2 * pair, 2)

        @pl.when(jnp.logical_and(has_next, pair == 0))
        def _():
            up(1, 1)

        @pl.when(jnp.logical_and(has_prev, pair < pairs - 1))
        def _():
            down(2 * pair, 2)

        @pl.when(jnp.logical_and(has_prev, pair == pairs - 1))
        def _():
            down(n - 2, 1)

    def landed(which, halo, way, pair, first, count):
        part = halo.at[pl.ds(first, count)]
        remote(part, part, halo_ss.at[which, way], halo_rs.at[which, way, pair], device(plane, mate)).wait_recv()

    def take_below(which, halo, pair, use):
        @pl.when(jnp.logical_and(has_prev, pair == 0))
        def _():
            landed(which, halo, 0, pair, 0, 1)
            use(0, halo.at[0])

        @pl.when(jnp.logical_and(has_prev, pair > 0))
        def _():
            landed(which, halo, 0, pair, 2 * pair - 1, 2)
            for r in range(2):
                use(2 * pair - 1 + r, halo.at[2 * pair - 1 + r])

    def take_above(which, halo, pair, use):
        @pl.when(jnp.logical_and(has_next, pair == pairs - 1))
        def _():
            landed(which, halo, 1, pair, 2 * n - 3, 1)
            use(3 * n - 3, halo.at[2 * n - 3])

        @pl.when(jnp.logical_and(has_next, pair < pairs - 1))
        def _():
            landed(which, halo, 1, pair, n - 1 + 2 * pair, 2)
            for r in range(2):
                use(2 * n - 1 + 2 * pair + r, halo.at[n - 1 + 2 * pair + r])

    def sent_up(which, halo):
        part = halo.at[pl.ds(0, n - 1)]
        remote(part, part, halo_ss.at[which, 0], halo_rs.at[which, 0], device(plane, mate)).wait_send()

    def sent_down(which, halo):
        part = halo.at[pl.ds(n - 1, n - 1)]
        remote(part, part, halo_ss.at[which, 1], halo_rs.at[which, 1], device(plane, mate)).wait_send()

    across = grp // 2
    fold_pair, grp_pair = mine // across, mine % across

    def to_pair(step):
        return (fold_pair + step // across) % fold * across + (grp_pair + step % across) % across

    def from_pair(step):
        return (fold_pair + fold - step // across) % fold * across + (grp_pair + across - step % across) % across

    def arrival(turn):
        return turn * across % (pairs - 1) + turn // (pairs - 1) * (pairs - 1)

    first_step = (fold - fold_pair) % fold * across + (across - grp_pair) % across

    def turn_order(turn):
        step = arrival(turn)
        other = jnp.where(step == 1, pairs - 1, jnp.where(step == pairs - 1, 1, step))
        return jnp.where(first_step == pairs - 1, other, step)

    def out_order(send):
        for turn in range(1, pairs):
            for r in (1, 0):
                send(2 * to_pair(arrival(turn)) + r)

    loads[0].wait()
    turn(k_in, k_src)
    pl.semaphore_wait(barrier, n - 1 + has_prev.astype(jnp.int32) + has_next.astype(jnp.int32))
    forward(0, k_halo, me, k_src.at[me])
    out_order(k_send)
    k_send(mate)
    loads[1].wait()
    turn(v_in, v_src)
    forward(1, v_halo, me, v_src.at[me], True)
    v_send(mate)
    loads[2].wait()
    turn(q_in, q_src)
    q_send(mate)
    out_order(v_send)
    def natural(slot, src):
        kn[slot] = src[...].T

    loads[3].wait()
    factor = math.log2(math.e) / math.sqrt(HDIM)
    blocks = img.shape[0]
    base = plane * n

    def span(block):
        own_id = img[block]
        before, after = jnp.int32(0), jnp.int32(0)
        for d in range(1, MOST):
            low = jnp.where(block >= d, img[jnp.maximum(block - d, 0)], -1)
            high = jnp.where(block + d < blocks, img[jnp.minimum(block + d, blocks - 1)], -1)
            before += (low == own_id).astype(jnp.int32)
            after += (high == own_id).astype(jnp.int32)
        return before, before + after + 1

    def note_span(m, carry):
        before, count = span(base + m)
        start_scr[m] = m + n - 1 - before
        count_scr[m] = count
        return carry

    lax.fori_loop(0, n, note_span, 0)
    natural(n - 1 + me, k_src.at[me])
    vt[n - 1 + me] = v_src[me]
    k_mate()
    forward(0, k_halo, mate, k_own.at[mate])
    v_mate()
    forward(1, v_halo, mate, v_own.at[mate], True)
    natural(n - 1 + mate, k_own.at[mate])
    vt[n - 1 + mate] = v_own[mate]
    def take_k(step, carry):
        pair = from_pair(arrival(step))
        k_take(pair)
        forward_pair(0, k_halo, pair, k_own)
        for r in range(2):
            natural(n - 1 + 2 * pair + r, k_own.at[2 * pair + r])
        return carry

    lax.fori_loop(1, pairs, take_k, 0)
    out_order(q_send)
    def take_v(step, carry):
        pair = from_pair(turn_order(step))
        v_take(pair)
        forward_pair(1, v_halo, pair, v_own)
        for r in range(2):
            vt[n - 1 + 2 * pair + r] = v_own[2 * pair + r]
        return carry

    lax.fori_loop(1, pairs, take_v, 0)
    def k_far(step, carry):
        take_below(0, k_halo, from_pair(arrival(step)), natural)
        take_above(0, k_halo, from_pair(arrival(step)), natural)
        return carry

    lax.fori_loop(0, pairs, k_far, 0)
    def scores(m, s_ref):
        start, count = start_scr[m], count_scr[m]
        rows = []
        for h in range(heads):
            q_h = q_own[m, h * HDIM:(h + 1) * HDIM]
            none = jnp.zeros_like(q_h)
            rows.append(jnp.concatenate([q_h if j == h else none for j in range(heads)], axis=1))
        q_all = jnp.concatenate(rows, axis=0)
        top = jnp.full((8, heads * BLK), NEG, jnp.float32)
        for t in range(MOST):
            s = jnp.dot(kn[start + jnp.where(t < count, t, 0)], q_all, preferred_element_type=jnp.float32)
            s_ref[t] = s
            high = jnp.max(s.reshape(BLK // 8, 8, heads * BLK), axis=0)
            top = jnp.maximum(top, jnp.where(t < count, high, NEG))
        return jnp.max(top, axis=0, keepdims=True), count

    def weigh(m, s_ref, top, count):
        total = jnp.zeros((8, heads * BLK), jnp.float32)
        for t in range(MOST):
            shift = jnp.where(t < count, -top * factor, NEG)
            w = jnp.exp2(s_ref[t] * factor + shift)
            total = total + jnp.sum(w.reshape(BLK // 8, 8, heads * BLK), axis=0)
            p_scr[m, t * BLK:(t + 1) * BLK] = w.astype(jnp.bfloat16)
        l_scr[m] = jnp.sum(total, axis=0, keepdims=True)

    def hold(slot, src):
        vt[slot] = src[...]

    _, _, _, _, o_sent = exchange(o_src, o_own, send_s.at[1], o_rs)

    def o_send(to):
        away = (to // grp + fold - fold_at) % fold
        remote(o_src.at[to], o_own.at[me], send_s.at[1], o_rs.at[(away + fold - 1) // fold],
               device(plane, to)).start()


    def finish(pair, local=False, lead=0):
        for r in range(2):
            m = 2 * pair + r
            start, count = start_scr[m], count_scr[m]
            v = jnp.concatenate([vt[start + jnp.where(t < count, t, 0)] for t in range(MOST)], axis=1)
            res = jnp.dot(v, p_scr[m], preferred_element_type=jnp.float32)
            res = jnp.concatenate([res[h * HDIM:(h + 1) * HDIM, h * BLK:(h + 1) * BLK]
                                   / l_scr[m, :, h * BLK:(h + 1) * BLK] for h in range(heads)], axis=0)
            o_src[m] = res.astype(jnp.bfloat16)
        if not local:
            for r in range(2):
                o_send(2 * pair + (lead + r) % 2)

    q_own[me] = q_src[me]
    q_mate()
    pair = from_pair(0)
    now = scores(2 * pair, s_scr.at[0])
    for step in range(pairs):
        if step < pairs - 1:
            coming = from_pair(turn_order(step + 1))
            q_take(coming)
        later = scores(2 * pair + 1, s_scr.at[1])
        weigh(2 * pair, s_scr.at[0], *now)
        if step < pairs - 1:
            now = scores(2 * coming, s_scr.at[0])
        weigh(2 * pair + 1, s_scr.at[1], *later)
        pair = coming
        if step == pairs - 2:
            @pl.when(jnp.logical_not(has_prev))
            def _():
                take_above(1, v_halo, 0, hold)

                @pl.when(mine != 0)
                def _():
                    finish(0)
    @pl.when(has_prev)
    def _():
        for pair in range(pairs):
            take_below(1, v_halo, pair, hold)
        take_above(1, v_halo, 0, hold)

        @pl.when(mine != 0)
        def _():
            finish(0, lead=0)

    def leave(pair, carry):
        take_above(1, v_halo, pair, hold)

        @pl.when(pair != mine)
        def _():
            finish(pair, lead=me)
        return carry

    lax.fori_loop(1, pairs, leave, 0)
    finish(mine, True)
    o_send(mate)
    o_own[me] = o_src[me]
    part = vt.at[pl.ds(0, 3 * n - 3)]
    remote(part, part, send_s.at[0], k_rs.at[0], device(plane, mate)).wait_send()
    for which, halo in ((0, k_halo), (1, v_halo)):
        @pl.when(has_next)
        def _():
            sent_up(which, halo)

        @pl.when(has_prev)
        def _():
            sent_down(which, halo)
    half = n // fold
    width = half * cols

    def settle(which, count):
        part = o_own.at[pl.ds(0, count)]
        remote(part, part, send_s.at[1], o_rs.at[which], device(plane, mate)).wait_recv()
        for f in range(1, fold) if which else range(1):
            at = (fold_at + f) % fold
            flat = jnp.concatenate([o_own[at * half + i] for i in range(half)], axis=0)
            for c in range(0, width, BLK):
                out[:, pl.ds(pl.multiple_of(at * width + c, BLK), BLK)] = flat[c:c + BLK].T

    settle(0, half - 1)
    settle(1, n - half)
    o_sent()


def solution(mesh):
    wide, grp = mesh.shape["wide"], mesh.shape["grp"]
    fold = MOST // grp
    n = fold * grp
    planes = wide // fold

    def body(query_rows, key_rows, value_rows, block_image):
        rows, width = query_rows.shape
        heads = width // HDIM // n
        cols = heads * HDIM
        bf, f32 = jnp.bfloat16, jnp.float32
        hbm = pl.BlockSpec(memory_space=pltpu.HBM)
        dma = pltpu.SemaphoreType.DMA
        slices = pltpu.VMEM((n, cols, BLK), bf)
        halo = pltpu.VMEM((2 * n - 2, cols, BLK), bf)
        lanes = heads * BLK
        args = [pltpu.with_memory_space_constraint(a, pltpu.HBM)
                for a in (block_image, query_rows, key_rows, value_rows)]
        return pl.pallas_call(
            functools.partial(kernel, (planes, fold, grp, heads)),
            out_shape=jax.ShapeDtypeStruct((rows, width), bf),
            in_specs=[hbm] * 4,
            out_specs=pl.BlockSpec(memory_space=pltpu.VMEM),
            scratch_shapes=[pltpu.SMEM(block_image.shape, jnp.int32)]
            + [pltpu.VMEM((rows, width), bf)] * 3 + [slices] * 6 + [halo] * 2 + [
                pltpu.VMEM((3 * n - 2, BLK, cols), bf),
                pltpu.VMEM((3 * n - 2, cols, BLK), bf),
                pltpu.VMEM((n, 1, lanes), f32),
                pltpu.VMEM((4, MOST, BLK, lanes), f32),
                pltpu.VMEM((n, MOST * BLK, lanes), bf),
                pltpu.SMEM((n,), jnp.int32), pltpu.SMEM((n,), jnp.int32),
                slices, slices,
            ] + [dma((4,))] + [dma((n // 2,))] * 3 + [dma((2,)), dma((2,)), dma((2, 2)), dma((2, 2, n // 2))],
            compiler_params=pltpu.CompilerParams(collective_id=0, has_side_effects=True,
                                                 vmem_limit_bytes=40 << 20),
        )(*args)

    return jax.shard_map(
        body,
        mesh=mesh,
        in_specs=(
            P(("wide", "grp"), None),
            P(("wide", "grp"), None),
            P(("wide", "grp"), None),
            P(),
        ),
        out_specs=P(("wide", "grp"), None),
        check_vma=False,
    )
```
